32 devices in a mesh: beam: 2 (over y), freq: 4 (over z), tm: 2 (over x), trial: 2 (over core).
Axes of the slice: x: 2, y: 2, z: 4, core: 2. Of those that a mesh axis runs over, the one named last changes fastest.
Arguments:
- spectra: bfloat16 [512, 2048], P(('beam', 'freq'), 'tm'), parts along dimension 0, may hold values from -6 to 6
- tap_offsets: int32 [4, 256, 64], P('freq'), may hold values from 0 to 31
- tap_weights: bfloat16 [4, 256, 64], P('freq'), may hold values from -0.375 to 0.375
- trial_map: int32 [4, 256], P('freq'), may hold values from 0 to 255
- delays: int32 [3, 256], replicated, may hold values from 0 to 32, as said below
Outputs:
- dedispersed: bfloat16 [512, 2048], P(('beam', 'freq', 'trial'), 'tm'), parts along dimension 0
The draws below stay inside these ranges and needn't reach their ends.
There are 2 independent parts, one for each index of `beam`. The reference program is written for one: setup_inputs(seed, part) draws one part's arguments, and reference() takes and returns one part's arrays. A program takes and returns all parts, laid end to end along the dimension named above; an argument that names none is the same for every part. Nothing has to cross between parts.
Inputs may be any that keep to these rules, and one draw needn't show every extreme that they name: delays[n, t] differs from t * 32 // 255 by at most 2, and equals 32 for the last trial of every merge.
All inputs are finite; a program needn't handle non-finite values.
Results may differ from the reference program's by a relative error of at most 0.0074.
Values may be sent and summed in bfloat16 or wider, within the bound.
No kernel may reach another device: no remote copies, remote signals or barrier semaphores. Data moves between devices by JAX's collectives and lax.ppermute only.
A program may use at most 64 MiB of HBM per device.

```python
import jax
import jax.numpy as jnp
from jax import lax

BAND = 64
TRIALS = 256
MAXOFF = 32
SHIFT = 32
SUBBANDS = 4
FREQS = 256
TIME = 2048
NODES = 3


def draw_delays(key, part):
    trial_ids = jnp.arange(TRIALS, dtype=jnp.int32)
    base_lag = trial_ids * SHIFT // (TRIALS - 1)
    jitter = jax.random.randint(key, (NODES, TRIALS), -2, 3, dtype=jnp.int32)
    lagged = jnp.clip(base_lag[None, :] + jitter, 0, SHIFT)
    return jnp.where(trial_ids[None, :] == TRIALS - 1, SHIFT, lagged).astype(jnp.int32)


def plant(values, rng, low, high):
    longest = values.shape.index(max(values.shape))
    spots = []
    for shift in (0, 1):
        where = [jax.random.randint(jax.random.fold_in(rng, axis), (), 0, length) for axis, length in enumerate(values.shape)]
        where[longest] = (where[longest] + shift) % values.shape[longest]
        spots.append(tuple(where))
    return values.at[spots[0]].set(low).at[spots[1]].set(high)


def block_scale(stream_key, extent, pieces, low, top_value):
    def one(position, blocks):
        draws = jax.random.uniform(jax.random.fold_in(jax.random.fold_in(stream_key, 6), position), (blocks,), jnp.float32, low / len(pieces), top_value / len(pieces))
        return jnp.repeat(jnp.exp(draws), extent[position] // blocks).reshape((-1,) + (1,) * (len(extent) - position - 1))

    gain = one(*pieces[0])
    for cut in pieces[1:]:
        gain = gain * one(*cut)
    return gain


def normal_values(own_key, shape, width, limit, cuts=(), kind=jnp.bfloat16):
    level = block_scale(own_key, shape, cuts, -0.22, 0.18) if cuts else 1.0
    array = jax.random.normal(own_key, shape, jnp.float32) * width * level
    return jnp.minimum(jnp.maximum(array, -limit), limit).astype(kind)


def setup_inputs(seed: int = 0, part: int = 0) -> dict:
    streams_of = jax.random.split(jax.random.key(seed), 6)
    part_keys = jax.random.split(jax.random.fold_in(streams_of[5], part), 6)
    spectra = normal_values(part_keys[0], (FREQS, TIME), 1.0, 6.0, ((0, 4), (1, 2)))
    tap_offsets = plant(jax.random.randint(streams_of[1], (SUBBANDS, TRIALS, BAND), 0, MAXOFF), jax.random.fold_in(streams_of[1], 1), 0, MAXOFF - 1).astype(jnp.int32)
    tap_weights = normal_values(streams_of[2], (SUBBANDS, TRIALS, BAND), (BAND * SUBBANDS) ** -0.5, 0.375, ((0, 4),))
    trial_map = plant(jax.random.randint(streams_of[3], (SUBBANDS, TRIALS), 0, TRIALS), jax.random.fold_in(streams_of[3], 1), 0, TRIALS - 1).astype(jnp.int32)
    delays = draw_delays(jax.random.fold_in(streams_of[5], 71), part)
    return {"spectra": spectra, "tap_offsets": tap_offsets, "tap_weights": tap_weights, "trial_map": trial_map, "delays": delays}


def leaf_plane(band_data, offsets, weights, chosen):
    length = band_data.shape[1] - MAXOFF
    offsets_sel = jnp.take(offsets, chosen, axis=0)
    weights_sel = jnp.take(weights, chosen, axis=0).astype(jnp.float32)
    window_index = jnp.arange(MAXOFF, dtype=jnp.int32)[:, None] + jnp.arange(length, dtype=jnp.int32)[None, :]

    def add_tap(tap_index, summed):
        channel = lax.dynamic_index_in_dim(band_data, tap_index, 0, keepdims=False)
        lagged = channel[window_index]
        column = lax.dynamic_index_in_dim(offsets_sel, tap_index, 1, keepdims=False)
        picked = jnp.take(lagged, column, axis=0)
        factor = lax.dynamic_index_in_dim(weights_sel, tap_index, 1, keepdims=False)
        return summed + factor[:, None] * picked

    summed = lax.fori_loop(0, BAND, add_tap, jnp.zeros((TRIALS, length), jnp.float32))
    return summed.astype(jnp.bfloat16)


def merge_pair(lower_plane, upper_plane, lag_values):
    length = lower_plane.shape[1]
    upper_padded = jnp.pad(upper_plane.astype(jnp.float32), ((0, 0), (0, SHIFT)))
    sample_index = lag_values[:, None].astype(jnp.int32) + jnp.arange(length, dtype=jnp.int32)[None, :]
    delayed = jnp.take_along_axis(upper_padded, sample_index, axis=1)
    return (lower_plane.astype(jnp.float32) + delayed).astype(jnp.bfloat16)


def reference(spectra, tap_offsets, tap_weights, trial_map, delays):
    padded = jnp.pad(spectra.astype(jnp.float32), ((0, 0), (0, MAXOFF)))
    pending = []
    for first in range(SUBBANDS):
        plane = leaf_plane(padded[first * BAND:(first + 1) * BAND], tap_offsets[first], tap_weights[first], trial_map[first])
        span_level = 0
        start = first
        while pending and pending[-1][1] == span_level:
            entry = pending.pop()
            node_index = SUBBANDS - (SUBBANDS >> span_level) + (entry[2] >> (span_level + 1))
            plane = merge_pair(entry[0], plane, delays[node_index])
            start = entry[2]
            span_level = span_level + 1
        pending.append((plane, span_level, start))
    return pending[0][0]
```

```python
import functools

import jax
import jax.numpy as jnp
from jax import lax
from jax.experimental import pallas as pl
from jax.experimental.pallas import tpu as pltpu
from jax.sharding import PartitionSpec as P

MAXOFF = 32
SHIFT = 32
LANES = 128


def bit_reversed(count):
    order = [0]
    while len(order) < count:
        order = [2 * r for r in order] + [2 * r + 1 for r in order]
    return order


def leaf_kernel(
    freq_count, halo, x_ref, off_ref, wt_ref, map_ref, del_ref, keep_ref, send_ref, xpad_ref, stack_ref, col_ref
):
    band, seg = x_ref.shape
    trials = map_ref.shape[1]
    wide = halo + seg
    row_block = trials // (2 * freq_count)
    rows = freq_count * row_block
    levels = freq_count.bit_length() - 1
    freq_index = lax.axis_index("freq")
    core_index = lax.axis_index("trial")

    total = jnp.zeros((1, trials), jnp.int32)
    for level in range(levels):
        node = freq_count - (freq_count >> level) + lax.shift_right_logical(freq_index, level + 1)
        bit = lax.shift_right_logical(freq_index, level) & 1
        total = total + del_ref[pl.ds(node, 1), :] * bit
    wide_map = jnp.broadcast_to(map_ref[...], (8, trials))
    wide_total = jnp.broadcast_to(total, (8, trials))
    first = lax.broadcasted_iota(jnp.int32, (8, trials), 0) == 0
    col_ref[...] = jnp.transpose(jnp.where(first, wide_map, wide_total).astype(jnp.float32))
    blocks = []
    for r in bit_reversed(freq_count):
        start = ((freq_index ^ r) * 2 + core_index) * row_block
        blocks.append(col_ref[pl.ds(pl.multiple_of(start, row_block), row_block), :])
    cols = jnp.concatenate(blocks, axis=0)
    chosen = cols[:, 0:1].astype(jnp.int32)
    lag = cols[:, 1:2].astype(jnp.int32)

    picker = (chosen == lax.broadcasted_iota(jnp.int32, (rows, trials), 1)).astype(jnp.float32).astype(jnp.bfloat16)
    wt = wt_ref[0]
    off = off_ref[0].astype(jnp.float32).astype(jnp.bfloat16)
    copies = LANES // band
    wt_rows = jnp.dot(picker, jnp.concatenate([wt] * copies, axis=1), preferred_element_type=jnp.float32)
    off_rows = jnp.dot(picker, jnp.concatenate([off] * copies, axis=1), preferred_element_type=jnp.float32).astype(
        jnp.int32
    )
    sub_lag = lax.broadcasted_iota(jnp.int32, (rows, LANES), 1) // band
    off_rows = off_rows - sub_lag

    xpad_ref[:, :halo] = jnp.zeros((band, halo), jnp.bfloat16)
    xpad_ref[:, halo : halo + seg] = x_ref[...]
    xpad_ref[:, halo + seg :] = jnp.zeros((band, LANES), jnp.bfloat16)
    padded = xpad_ref[...]
    for d in range(MAXOFF):
        if d:
            moved = pltpu.roll(padded, wide + LANES - d, 1)[:, :wide]
        else:
            moved = padded[:, :wide]
        stack_ref[d * band : (d + 1) * band, :] = moved
    pieces = []
    for first_lag in range(0, MAXOFF, copies):
        pieces.append(jnp.where(off_rows == first_lag, wt_rows, 0.0).astype(jnp.bfloat16))
    kernel = jnp.concatenate(pieces, axis=1)
    leaf = jnp.dot(kernel, stack_ref[...], preferred_element_type=jnp.float32).astype(jnp.bfloat16)
    leaf = jnp.concatenate([leaf, jnp.zeros((rows, halo), jnp.bfloat16)], axis=1)

    span = levels * SHIFT
    step = 1
    while step <= span:
        moved = pltpu.roll(leaf, wide + halo - step, 1)
        leaf = jnp.where((lag & step) != 0, moved, leaf)
        step *= 2
    half = rows // 2
    keep_ref[...] = leaf[:half, :wide]
    send_ref[...] = leaf[half:, :wide]


def add_bf16(a, b):
    return (a.astype(jnp.float32) + b.astype(jnp.float32)).astype(jnp.bfloat16)


def merge_kernel(keep_ref, recv_ref, low_ref, high_ref):
    half = low_ref.shape[0]
    low_ref[...] = add_bf16(keep_ref[:half, :], recv_ref[:half, :])
    high_ref[...] = add_bf16(keep_ref[half:, :], recv_ref[half:, :])


def split_kernel(halo, keep_ref, recv_ref, low_ref, low_halo_ref, high_ref, high_halo_ref):
    half = low_ref.shape[0]
    low = add_bf16(keep_ref[:half, :], recv_ref[:half, :])
    low_halo_ref[...] = low[:, :halo]
    low_ref[...] = low[:, halo:]
    high = add_bf16(keep_ref[half:, :], recv_ref[half:, :])
    high_halo_ref[...] = high[:, :halo]
    high_ref[...] = high[:, halo:]


def final_kernel(keep_ref, recv_ref, keep_halo_ref, recv_halo_ref, out_ref):
    seg = out_ref.shape[1]
    halo = keep_halo_ref.shape[1]
    body = seg - halo
    out_ref[:, :body] = add_bf16(keep_ref[:, :body], recv_ref[:, :body])
    lower = keep_ref[:, body:].astype(jnp.float32) + keep_halo_ref[...].astype(jnp.float32)
    upper = recv_ref[:, body:].astype(jnp.float32) + recv_halo_ref[...].astype(jnp.float32)
    out_ref[:, body:] = (lower + upper).astype(jnp.bfloat16)


def call(kernel, shapes, *args, scratch=(), limit=16 << 20):
    outs = [jax.ShapeDtypeStruct(shape, jnp.bfloat16) for shape in shapes]
    return pl.pallas_call(
        kernel,
        out_shape=outs,
        scratch_shapes=list(scratch),
        compiler_params=pltpu.CompilerParams(vmem_limit_bytes=limit),
    )(*args)


def shards(spectra, tap_offsets, tap_weights, trial_map, delays):
    band, seg = spectra.shape
    trials = trial_map.shape[1]
    freq_count = lax.axis_size("freq")
    tm_count = lax.axis_size("tm")
    levels = freq_count.bit_length() - 1
    rows = trials // 2
    halo = -(-(MAXOFF - 1 + levels * SHIFT) // LANES) * LANES
    wide = halo + seg

    scratch = (
        pltpu.VMEM((band, wide + LANES), jnp.bfloat16),
        pltpu.VMEM((MAXOFF * band, wide), jnp.bfloat16),
        pltpu.VMEM((trials, 8), jnp.float32),
    )
    keep, send = call(
        functools.partial(leaf_kernel, freq_count, halo),
        [(rows // 2, wide)] * 2,
        spectra,
        tap_offsets,
        tap_weights,
        trial_map,
        delays,
        scratch=scratch,
        limit=24 << 20,
    )
    for level in range(levels - 1):
        swap = [(i, i ^ (1 << level)) for i in range(freq_count)]
        recv = lax.ppermute(send, "freq", swap)
        half = keep.shape[0] // 2
        if level < levels - 2:
            keep, send = call(merge_kernel, [(half, wide)] * 2, keep, recv)
        else:
            low, low_halo, high, high_halo = call(
                functools.partial(split_kernel, halo), [(half, seg), (half, halo)] * 2, keep, recv
            )
    bit = 1 << (levels - 1)
    swap = [(i, i ^ bit) for i in range(freq_count)]
    recv = lax.ppermute(high, "freq", swap)
    back = [(m + 1, m) for m in range(tm_count - 1)]
    keep_halo = lax.ppermute(low_halo, "tm", back)
    cross = [((i ^ bit) * tm_count + m + 1, i * tm_count + m) for i in range(freq_count) for m in range(tm_count - 1)]
    recv_halo = lax.ppermute(high_halo, ("freq", "tm"), cross)
    (out,) = call(final_kernel, [low.shape], low, recv, keep_halo, recv_halo)
    return out


def solution(mesh):
    return jax.shard_map(
        shards,
        mesh=mesh,
        in_specs=(
            P(("beam", "freq"), "tm"),
            P("freq", None, None),
            P("freq", None, None),
            P("freq", None),
            P(),
        ),
        out_specs=P(("beam", "freq", "trial"), "tm"),
        check_vma=False,
    )
```

```python
import functools

import jax
import jax.numpy as jnp
from jax import lax
from jax.experimental import pallas as pl
from jax.experimental.pallas import tpu as pltpu
from jax.sharding import PartitionSpec as P

MAXOFF = 32
SHIFT = 32
LANES = 128
FINE = 8
PLANES = (MAXOFF - 1 + FINE - 1) // FINE + 1


def bit_reversed(count):
    order = [0]
    while len(order) < count:
        order = [2 * r for r in order] + [2 * r + 1 for r in order]
    return order


def own_columns(freq_count, map_ref, del_ref):
    trials = map_ref.shape[1]
    row_block = trials // (2 * freq_count)
    rows = trials // 2
    levels = freq_count.bit_length() - 1
    freq_index = lax.axis_index("freq")
    core_index = lax.axis_index("trial")
    total = jnp.zeros((1, trials), jnp.int32)
    for level in range(levels):
        node = freq_count - (freq_count >> level) + lax.shift_right_logical(freq_index, level + 1)
        bit = lax.shift_right_logical(freq_index, level) & 1
        total = total + del_ref[pl.ds(node, 1), :] * bit
    first = lax.broadcasted_iota(jnp.int32, (8, trials), 0) == 0
    both = jnp.where(
        first, jnp.broadcast_to(map_ref[...], (8, trials)), jnp.broadcast_to(total, (8, trials))
    )
    place = lax.broadcasted_iota(jnp.int32, (8, rows), 1) // row_block
    mine = jnp.zeros((8, rows), jnp.int32)
    for position, r in enumerate(bit_reversed(freq_count)):
        start = ((freq_index ^ r) * 2 + core_index) * row_block
        turn = lax.rem(position * row_block - start + trials, trials)
        mine = jnp.where(place == position, pltpu.roll(both, turn, 1)[:, :rows], mine)
    return mine


def build_taps(off_ref, wt_ref, mine, rhs_ref):
    band, trials = wt_ref.shape
    rows = mine.shape[1]
    picker = mine[0:1, :] == lax.broadcasted_iota(jnp.int32, (trials, rows), 0)
    picker = picker.astype(jnp.float32).astype(jnp.bfloat16)
    tables = jnp.concatenate([wt_ref[...], off_ref[...].astype(jnp.float32).astype(jnp.bfloat16)], axis=0)
    picked = jnp.dot(tables, picker, preferred_element_type=jnp.float32)
    weights = picked[:band]
    lags = picked[band:].astype(jnp.int32) + (mine[1:2, :] & (FINE - 1))
    for fine in range(FINE):
        for plane in range(PLANES):
            rhs_ref[fine * band : (fine + 1) * band, plane * rows : (plane + 1) * rows] = jnp.where(
                lags == plane * FINE + fine, weights, 0.0
            ).astype(jnp.bfloat16)


def convolve(window, span, columns, delay_row, rhs_ref, time_ref, lhs_ref, plane_ref, leaf_ref):
    band = window.shape[0]
    rows = delay_row.shape[1]
    leaf_rows = columns + span
    lhs_rows = leaf_rows + FINE * (PLANES - 1)
    time_rows = lhs_rows + FINE
    turned = jnp.transpose(jnp.concatenate([window] * (LANES // band), axis=0).astype(jnp.float32))
    time_ref[:time_rows, :] = turned[:time_rows, :]
    low_lanes = lax.broadcasted_iota(jnp.int32, (lhs_rows, LANES), 1) < band
    for pair in range(FINE // 2):
        lhs_ref[:lhs_rows, pair * LANES : (pair + 1) * LANES] = jnp.where(
            low_lanes,
            time_ref[2 * pair : 2 * pair + lhs_rows, :],
            time_ref[2 * pair + 1 : 2 * pair + 1 + lhs_rows, :],
        ).astype(jnp.bfloat16)
    plane_ref[:lhs_rows, :] = jnp.dot(lhs_ref[:lhs_rows, :], rhs_ref[...], preferred_element_type=jnp.float32)
    leaf = plane_ref[:leaf_rows, :rows]
    for plane in range(1, PLANES):
        leaf = leaf + plane_ref[plane * FINE : plane * FINE + leaf_rows, plane * rows : (plane + 1) * rows]
    leaf_ref[:leaf_rows, :] = leaf
    steps = [FINE]
    while steps[-1] * 2 <= span:
        steps.append(steps[-1] * 2)
    blocks = []
    for start in range(0, columns, LANES):
        part = leaf_ref[start : start + LANES + span, :]
        for step in reversed(steps):
            length = LANES + sum(s for s in steps if s < step)
            length = min(length, part.shape[0])
            take = jnp.broadcast_to((delay_row & step) != 0, (length, rows))
            moved = part[step : step + length]
            if moved.shape[0] < length:
                moved = jnp.concatenate([moved, jnp.zeros((length - moved.shape[0], rows), jnp.float32)], axis=0)
            part = jnp.where(take, moved, part[:length])
        blocks.append(jnp.transpose(part[:LANES]).astype(jnp.bfloat16))
    return blocks


def main_kernel(
    freq_count, tail, x_ref, off_ref, wt_ref, map_ref, del_ref,
    keep_ref, send_ref, rhs_ref, delay_ref, time_ref, lhs_ref, plane_ref, leaf_ref,
):
    mine = own_columns(freq_count, map_ref, del_ref)
    build_taps(off_ref, wt_ref, mine, rhs_ref)
    delay_ref[...] = mine
    columns = keep_ref.shape[1]
    span = (freq_count.bit_length() - 1) * SHIFT
    half = keep_ref.shape[0]
    blocks = convolve(x_ref[...], span, columns, mine[1:2, :], rhs_ref, time_ref, lhs_ref, plane_ref, leaf_ref)
    for index, block in enumerate(blocks):
        keep_ref[:, index * LANES : (index + 1) * LANES] = block[:half]
        send_ref[:, index * LANES : (index + 1) * LANES] = block[half:]


def tail_kernel(
    freq_count, tail, x_ref, next_ref, rhs_ref, delay_ref, keep_in_ref, send_in_ref,
    keep_ref, send_ref, time_ref, lhs_ref, plane_ref, leaf_ref,
):
    seg = x_ref.shape[1]
    body = seg - tail
    half = keep_ref.shape[0]
    span = (freq_count.bit_length() - 1) * SHIFT
    window = jnp.concatenate([x_ref[:, body:], next_ref[...]], axis=1)
    blocks = convolve(window, span, tail, delay_ref[1:2, :], rhs_ref, time_ref, lhs_ref, plane_ref, leaf_ref)
    keep_ref[:, :body] = keep_in_ref[...]
    send_ref[:, :body] = send_in_ref[...]
    for index, block in enumerate(blocks):
        place = slice(body + index * LANES, body + (index + 1) * LANES)
        keep_ref[:, place] = block[:half]
        send_ref[:, place] = block[half:]


def add_bf16(a, b):
    return (a.astype(jnp.float32) + b.astype(jnp.float32)).astype(jnp.bfloat16)


def merge_kernel(keep_ref, recv_ref, low_ref, high_ref):
    half = low_ref.shape[0]
    low_ref[...] = add_bf16(keep_ref[:half, :], recv_ref[:half, :])
    high_ref[...] = add_bf16(keep_ref[half:, :], recv_ref[half:, :])


def final_kernel(keep_ref, recv_ref, out_ref):
    out_ref[...] = add_bf16(keep_ref[...], recv_ref[...])


def call(kernel, outs, *args, scratch=(), limit=16 << 20):
    return pl.pallas_call(
        kernel,
        out_shape=outs,
        scratch_shapes=list(scratch),
        compiler_params=pltpu.CompilerParams(vmem_limit_bytes=limit),
    )(*args)


def plane_of(*shape):
    return jax.ShapeDtypeStruct(shape, jnp.bfloat16)


def shards(spectra, tap_offsets, tap_weights, trial_map, delays):
    band, seg = spectra.shape
    trials = trial_map.shape[1]
    freq_count = lax.axis_size("freq")
    tm_count = lax.axis_size("tm")
    levels = freq_count.bit_length() - 1
    rows = trials // 2
    half = rows // 2
    span = levels * SHIFT
    tail = -(-(MAXOFF - 1 + span) // LANES) * LANES
    body = seg - tail

    def scratch(columns):
        leaf_rows = columns + span
        lhs_rows = leaf_rows + FINE * (PLANES - 1)
        return (
            pltpu.VMEM((lhs_rows + FINE, LANES), jnp.float32),
            pltpu.VMEM((lhs_rows, FINE * band), jnp.bfloat16),
            pltpu.VMEM((lhs_rows, PLANES * rows), jnp.float32),
            pltpu.VMEM((leaf_rows, rows), jnp.float32),
        )

    back = [(m + 1, m) for m in range(tm_count - 1)]
    following = lax.ppermute(spectra[:, :tail], "tm", back)
    keep, send, taps, columns = call(
        functools.partial(main_kernel, freq_count, tail),
        [plane_of(half, body)] * 2
        + [plane_of(FINE * band, PLANES * rows), jax.ShapeDtypeStruct((8, rows), jnp.int32)],
        spectra,
        jnp.swapaxes(tap_offsets[0], 0, 1),
        jnp.swapaxes(tap_weights[0], 0, 1),
        trial_map,
        delays,
        scratch=scratch(body),
    )
    keep, send = call(
        functools.partial(tail_kernel, freq_count, tail),
        [plane_of(half, seg)] * 2,
        spectra,
        following,
        taps,
        columns,
        keep,
        send,
        scratch=scratch(tail),
    )
    for level in range(levels):
        swap = [(i, i ^ (1 << level)) for i in range(freq_count)]
        recv = lax.ppermute(send, "freq", swap)
        if level < levels - 1:
            half = keep.shape[0] // 2
            keep, send = call(merge_kernel, [plane_of(half, seg)] * 2, keep, recv)
    return call(final_kernel, plane_of(*keep.shape), keep, recv)


def solution(mesh):
    return jax.shard_map(
        shards,
        mesh=mesh,
        in_specs=(
            P(("beam", "freq"), "tm"),
            P("freq", None, None),
            P("freq", None, None),
            P("freq", None),
            P(),
        ),
        out_specs=P(("beam", "freq", "trial"), "tm"),
        check_vma=False,
    )
```

```python
import functools

import jax
import jax.numpy as jnp
from jax import lax
from jax.experimental import pallas as pl
from jax.experimental.pallas import tpu as pltpu
from jax.sharding import PartitionSpec as P

MAXOFF = 32
SHIFT = 32
LANES = 128
FINE = 8
PLANES = (MAXOFF - 1 + FINE - 1) // FINE + 1


def bit_reversed(count):
    order = [0]
    while len(order) < count:
        order = [2 * r for r in order] + [2 * r + 1 for r in order]
    return order


def own_columns(freq_count, map_ref, del_ref):
    trials = map_ref.shape[1]
    row_block = trials // (2 * freq_count)
    rows = trials // 2
    levels = freq_count.bit_length() - 1
    freq_index = lax.axis_index("freq")
    core_index = lax.axis_index("trial")
    total = jnp.zeros((1, trials), jnp.int32)
    for level in range(levels):
        node = freq_count - (freq_count >> level) + lax.shift_right_logical(freq_index, level + 1)
        bit = lax.shift_right_logical(freq_index, level) & 1
        total = total + del_ref[pl.ds(node, 1), :] * bit
    first = lax.broadcasted_iota(jnp.int32, (8, trials), 0) == 0
    both = jnp.where(
        first, jnp.broadcast_to(map_ref[...], (8, trials)), jnp.broadcast_to(total, (8, trials))
    )
    place = lax.broadcasted_iota(jnp.int32, (8, rows), 1) // row_block
    mine = jnp.zeros((8, rows), jnp.int32)
    for position, r in enumerate(bit_reversed(freq_count)):
        start = ((freq_index ^ r) * 2 + core_index) * row_block
        turn = lax.rem(position * row_block - start + trials, trials)
        mine = jnp.where(place == position, pltpu.roll(both, turn, 1)[:, :rows], mine)
    return mine


def build_taps(off_ref, wt_ref, mine, rhs_ref):
    band, trials = wt_ref.shape
    rows = mine.shape[1]
    picker = mine[0:1, :] == lax.broadcasted_iota(jnp.int32, (trials, rows), 0)
    picker = picker.astype(jnp.float32).astype(jnp.bfloat16)
    tables = jnp.concatenate([wt_ref[...], off_ref[...].astype(jnp.float32).astype(jnp.bfloat16)], axis=0)
    picked = jnp.dot(tables, picker, preferred_element_type=jnp.float32)
    weights = picked[:band]
    lags = picked[band:].astype(jnp.int32) + (mine[1:2, :] & (FINE - 1))
    for fine in range(FINE):
        for plane in range(PLANES):
            rhs_ref[fine * band : (fine + 1) * band, plane * rows : (plane + 1) * rows] = jnp.where(
                lags == plane * FINE + fine, weights, 0.0
            ).astype(jnp.bfloat16)


def convolve(window, span, columns, delay_row, rhs_ref, time_ref, lhs_ref, plane_ref, leaf_ref):
    band = window.shape[0]
    rows = delay_row.shape[1]
    leaf_rows = columns + span
    lhs_rows = leaf_rows + FINE * (PLANES - 1)
    time_rows = lhs_rows + FINE
    turned = jnp.transpose(jnp.concatenate([window] * (LANES // band), axis=0).astype(jnp.float32))
    time_ref[:time_rows, :] = turned[:time_rows, :]
    low_lanes = lax.broadcasted_iota(jnp.int32, (lhs_rows, LANES), 1) < band
    for pair in range(FINE // 2):
        lhs_ref[:lhs_rows, pair * LANES : (pair + 1) * LANES] = jnp.where(
            low_lanes,
            time_ref[2 * pair : 2 * pair + lhs_rows, :],
            time_ref[2 * pair + 1 : 2 * pair + 1 + lhs_rows, :],
        ).astype(jnp.bfloat16)
    plane_ref[:lhs_rows, :] = jnp.dot(lhs_ref[:lhs_rows, :], rhs_ref[...], preferred_element_type=jnp.float32)
    leaf = plane_ref[:leaf_rows, :rows]
    for plane in range(1, PLANES):
        leaf = leaf + plane_ref[plane * FINE : plane * FINE + leaf_rows, plane * rows : (plane + 1) * rows]
    leaf_ref[:leaf_rows, :] = leaf
    steps = [FINE]
    while steps[-1] * 2 <= span:
        steps.append(steps[-1] * 2)
    blocks = []
    for start in range(0, columns, LANES):
        part = leaf_ref[start : start + LANES + span, :]
        for step in reversed(steps):
            length = LANES + sum(s for s in steps if s < step)
            length = min(length, part.shape[0])
            take = jnp.broadcast_to((delay_row & step) != 0, (length, rows))
            moved = part[step : step + length]
            if moved.shape[0] < length:
                moved = jnp.concatenate([moved, jnp.zeros((length - moved.shape[0], rows), jnp.float32)], axis=0)
            part = jnp.where(take, moved, part[:length])
        blocks.append(jnp.transpose(part[:LANES]).astype(jnp.bfloat16))
    return blocks


def main_kernel(
    freq_count, tail, x_hbm, off_hbm, wt_hbm, map_hbm, del_hbm,
    keep_ref, send_ref, rhs_ref, delay_ref, x_ref,
    off_ref, wt_ref, map_ref, del_ref, time_ref, lhs_ref, plane_ref, leaf_ref, sems,
):
    moves = [
        pltpu.make_async_copy(source, target, sems.at[index])
        for index, (source, target) in enumerate(
            ((map_hbm, map_ref), (del_hbm, del_ref), (wt_hbm, wt_ref), (off_hbm, off_ref), (x_hbm, x_ref))
        )
    ]
    for move in moves:
        move.start()
    moves[0].wait()
    moves[1].wait()
    mine = own_columns(freq_count, map_ref, del_ref)
    moves[2].wait()
    moves[3].wait()
    build_taps(off_ref, wt_ref, mine, rhs_ref)
    moves[4].wait()
    delay_ref[...] = mine
    columns = keep_ref.shape[1]
    span = (freq_count.bit_length() - 1) * SHIFT
    half = keep_ref.shape[0]
    blocks = convolve(x_ref[...], span, columns, mine[1:2, :], rhs_ref, time_ref, lhs_ref, plane_ref, leaf_ref)
    for index, block in enumerate(blocks):
        keep_ref[:, index * LANES : (index + 1) * LANES] = block[:half]
        send_ref[:, index * LANES : (index + 1) * LANES] = block[half:]


def tail_kernel(
    freq_count, tail, tm_count, x_ref, next_ref, rhs_ref, delay_ref, keep_in_ref, send_in_ref,
    keep_ref, send_ref, time_ref, lhs_ref, plane_ref, leaf_ref,
):
    seg = x_ref.shape[1]
    body = seg - tail
    half = keep_ref.shape[0]
    span = (freq_count.bit_length() - 1) * SHIFT
    inside = lax.axis_index("tm") < tm_count - 1
    following = jnp.where(inside, next_ref[:, :tail].astype(jnp.float32), 0.0).astype(jnp.bfloat16)
    window = jnp.concatenate([x_ref[:, body:], following], axis=1)
    blocks = convolve(window, span, tail, delay_ref[1:2, :], rhs_ref, time_ref, lhs_ref, plane_ref, leaf_ref)
    keep_ref[:, :body] = keep_in_ref[...]
    send_ref[:, :body] = send_in_ref[...]
    for index, block in enumerate(blocks):
        place = slice(body + index * LANES, body + (index + 1) * LANES)
        keep_ref[:, place] = block[:half]
        send_ref[:, place] = block[half:]


def add_bf16(a, b):
    return (a.astype(jnp.float32) + b.astype(jnp.float32)).astype(jnp.bfloat16)


def merge_kernel(keep_ref, recv_ref, low_ref, high_ref):
    half = low_ref.shape[0]
    low_ref[...] = add_bf16(keep_ref[:half, :], recv_ref[:half, :])
    high_ref[...] = add_bf16(keep_ref[half:, :], recv_ref[half:, :])


def final_kernel(keep_ref, recv_ref, out_ref):
    out_ref[...] = add_bf16(keep_ref[...], recv_ref[...])


def call(kernel, outs, *args, scratch=(), limit=16 << 20, space=None):
    specs = {} if space is None else {"in_specs": [pl.BlockSpec(memory_space=space)] * len(args)}
    if space is not None:
        args = [pltpu.with_memory_space_constraint(arg, space) for arg in args]
    return pl.pallas_call(
        kernel,
        out_shape=outs,
        **specs,
        scratch_shapes=list(scratch),
        compiler_params=pltpu.CompilerParams(vmem_limit_bytes=limit),
    )(*args)


def plane_of(*shape):
    return jax.ShapeDtypeStruct(shape, jnp.bfloat16)


def shards(spectra, tap_offsets, tap_weights, trial_map, delays):
    band, seg = spectra.shape
    trials = trial_map.shape[1]
    freq_count = lax.axis_size("freq")
    tm_count = lax.axis_size("tm")
    levels = freq_count.bit_length() - 1
    rows = trials // 2
    half = rows // 2
    span = levels * SHIFT
    tail = -(-(MAXOFF - 1 + span) // LANES) * LANES
    body = seg - tail

    def scratch(columns):
        leaf_rows = columns + span
        lhs_rows = leaf_rows + FINE * (PLANES - 1)
        return (
            pltpu.VMEM((lhs_rows + FINE, LANES), jnp.float32),
            pltpu.VMEM((lhs_rows, FINE * band), jnp.bfloat16),
            pltpu.VMEM((lhs_rows, PLANES * rows), jnp.float32),
            pltpu.VMEM((leaf_rows, rows), jnp.float32),
        )

    ring = [((m + 1) % tm_count, m) for m in range(tm_count)]
    following = lax.ppermute(spectra, "tm", ring)
    keep, send, taps, columns, samples = call(
        functools.partial(main_kernel, freq_count, tail),
        [plane_of(half, body)] * 2
        + [
            plane_of(FINE * band, PLANES * rows),
            jax.ShapeDtypeStruct((8, rows), jnp.int32),
            plane_of(band, seg),
        ],
        spectra,
        jnp.swapaxes(tap_offsets[0], 0, 1),
        jnp.swapaxes(tap_weights[0], 0, 1),
        trial_map,
        delays,
        scratch=(
            pltpu.VMEM((band, trials), jnp.int32),
            pltpu.VMEM((band, trials), jnp.bfloat16),
            pltpu.VMEM((1, trials), jnp.int32),
            pltpu.VMEM(delays.shape, jnp.int32),
        )
        + scratch(body)
        + (pltpu.SemaphoreType.DMA((5,)),),
        space=pltpu.HBM,
    )
    keep, send = call(
        functools.partial(tail_kernel, freq_count, tail, tm_count),
        [plane_of(half, seg)] * 2,
        samples,
        following,
        taps,
        columns,
        keep,
        send,
        scratch=scratch(tail),
    )
    for level in range(levels):
        swap = [(i, i ^ (1 << level)) for i in range(freq_count)]
        recv = lax.ppermute(send, "freq", swap)
        if level < levels - 1:
            half = keep.shape[0] // 2
            keep, send = call(merge_kernel, [plane_of(half, seg)] * 2, keep, recv)
    return call(final_kernel, plane_of(*keep.shape), keep, recv)


def solution(mesh):
    return jax.shard_map(
        shards,
        mesh=mesh,
        in_specs=(
            P(("beam", "freq"), "tm"),
            P("freq", None, None),
            P("freq", None, None),
            P("freq", None),
            P(),
        ),
        out_specs=P(("beam", "freq", "trial"), "tm"),
        check_vma=False,
    )
```

```python
import functools

import jax
import jax.numpy as jnp
from jax import lax
from jax.experimental import pallas as pl
from jax.experimental.pallas import tpu as pltpu
from jax.sharding import PartitionSpec as P

MAXOFF = 32
SHIFT = 32
LANES = 128
FINE = 8
PLANES = (MAXOFF - 1 + FINE - 1) // FINE + 1


def bit_reversed(count):
    order = [0]
    while len(order) < count:
        order = [2 * r for r in order] + [2 * r + 1 for r in order]
    return order


def own_columns(freq_count, map_ref, del_ref):
    trials = map_ref.shape[1]
    row_block = trials // (2 * freq_count)
    rows = trials // 2
    levels = freq_count.bit_length() - 1
    freq_index = lax.axis_index("freq")
    core_index = lax.axis_index("trial")
    total = jnp.zeros((1, trials), jnp.int32)
    for level in range(levels):
        node = freq_count - (freq_count >> level) + lax.shift_right_logical(freq_index, level + 1)
        bit = lax.shift_right_logical(freq_index, level) & 1
        total = total + del_ref[pl.ds(node, 1), :] * bit
    first = lax.broadcasted_iota(jnp.int32, (8, trials), 0) == 0
    both = jnp.where(
        first, jnp.broadcast_to(map_ref[...], (8, trials)), jnp.broadcast_to(total, (8, trials))
    )
    place = lax.broadcasted_iota(jnp.int32, (8, rows), 1) // row_block
    mine = jnp.zeros((8, rows), jnp.int32)
    for position, r in enumerate(bit_reversed(freq_count)):
        start = ((freq_index ^ r) * 2 + core_index) * row_block
        turn = lax.rem(position * row_block - start + trials, trials)
        mine = jnp.where(place == position, pltpu.roll(both, turn, 1)[:, :rows], mine)
    return mine


def build_taps(off_ref, wt_ref, mine, rhs_ref):
    band, trials = wt_ref.shape
    rows = mine.shape[1]
    picker = mine[0:1, :] == lax.broadcasted_iota(jnp.int32, (trials, rows), 0)
    picker = picker.astype(jnp.float32).astype(jnp.bfloat16)
    tables = jnp.concatenate([wt_ref[...], off_ref[...].astype(jnp.float32).astype(jnp.bfloat16)], axis=0)
    picked = jnp.dot(tables, picker, preferred_element_type=jnp.float32)
    weights = picked[:band]
    lags = picked[band:].astype(jnp.int32) + (mine[1:2, :] & (FINE - 1))
    for fine in range(FINE):
        for plane in range(PLANES):
            rhs_ref[fine * band : (fine + 1) * band, plane * rows : (plane + 1) * rows] = jnp.where(
                lags == plane * FINE + fine, weights, 0.0
            ).astype(jnp.bfloat16)


def convolve(window, span, columns, delay_row, rhs_ref, time_ref, lhs_ref, plane_ref, leaf_ref):
    band = window.shape[0]
    rows = delay_row.shape[1]
    leaf_rows = columns + span
    lhs_rows = leaf_rows + FINE * (PLANES - 1)
    time_rows = lhs_rows + FINE
    turned = jnp.transpose(jnp.concatenate([window] * (LANES // band), axis=0).astype(jnp.float32))
    time_ref[:time_rows, :] = turned[:time_rows, :]
    low_lanes = lax.broadcasted_iota(jnp.int32, (lhs_rows, LANES), 1) < band
    for pair in range(FINE // 2):
        lhs_ref[:lhs_rows, pair * LANES : (pair + 1) * LANES] = jnp.where(
            low_lanes,
            time_ref[2 * pair : 2 * pair + lhs_rows, :],
            time_ref[2 * pair + 1 : 2 * pair + 1 + lhs_rows, :],
        ).astype(jnp.bfloat16)
    plane_ref[:lhs_rows, :] = jnp.dot(lhs_ref[:lhs_rows, :], rhs_ref[...], preferred_element_type=jnp.float32)
    leaf = plane_ref[:leaf_rows, :rows]
    for plane in range(1, PLANES):
        leaf = leaf + plane_ref[plane * FINE : plane * FINE + leaf_rows, plane * rows : (plane + 1) * rows]
    leaf_ref[:leaf_rows, :] = leaf
    steps = [FINE]
    while steps[-1] * 2 <= span:
        steps.append(steps[-1] * 2)
    blocks = []
    for start in range(0, columns, LANES):
        part = leaf_ref[start : start + LANES + span, :]
        for step in reversed(steps):
            length = LANES + sum(s for s in steps if s < step)
            length = min(length, part.shape[0])
            take = jnp.broadcast_to((delay_row & step) != 0, (length, rows))
            moved = part[step : step + length]
            if moved.shape[0] < length:
                moved = jnp.concatenate([moved, jnp.zeros((length - moved.shape[0], rows), jnp.float32)], axis=0)
            part = jnp.where(take, moved, part[:length])
        blocks.append(jnp.transpose(part[:LANES]).astype(jnp.bfloat16))
    return blocks


def load_kernel(x_hbm, off_hbm, wt_hbm, map_hbm, del_hbm, edge_ref, x_ref, off_ref, wt_ref, map_ref, del_ref, sems):
    moves = [
        pltpu.make_async_copy(source, target, sems.at[index])
        for index, (source, target) in enumerate(
            (
                (x_hbm.at[:, : edge_ref.shape[1]], edge_ref),
                (x_hbm, x_ref),
                (off_hbm, off_ref),
                (wt_hbm, wt_ref),
                (map_hbm, map_ref),
                (del_hbm, del_ref),
            )
        )
    ]
    for move in moves:
        move.start()
    for move in moves:
        move.wait()


def main_kernel(
    freq_count, x_ref, off_ref, wt_ref, map_ref, del_ref,
    body_ref, rhs_ref, delay_ref, time_ref, lhs_ref, plane_ref, leaf_ref,
):
    mine = own_columns(freq_count, map_ref, del_ref)
    build_taps(off_ref, wt_ref, mine, rhs_ref)
    delay_ref[...] = mine
    columns = body_ref.shape[1]
    span = (freq_count.bit_length() - 1) * SHIFT
    blocks = convolve(x_ref[...], span, columns, mine[1:2, :], rhs_ref, time_ref, lhs_ref, plane_ref, leaf_ref)
    for index, block in enumerate(blocks):
        body_ref[:, index * LANES : (index + 1) * LANES] = block


def tail_kernel(
    freq_count, tm_count, parts, x_ref, next_ref, rhs_ref, delay_ref, body_ref, *rest
):
    outs, (time_ref, lhs_ref, plane_ref, leaf_ref) = rest[:parts], rest[parts:]
    body = body_ref.shape[1]
    tail = x_ref.shape[1] - body
    piece = outs[0].shape[0]
    span = (freq_count.bit_length() - 1) * SHIFT
    inside = lax.axis_index("tm") < tm_count - 1
    following = jnp.where(inside, next_ref[...].astype(jnp.float32), 0.0).astype(jnp.bfloat16)
    window = jnp.concatenate([x_ref[:, body:], following], axis=1)
    blocks = convolve(window, span, tail, delay_ref[1:2, :], rhs_ref, time_ref, lhs_ref, plane_ref, leaf_ref)
    for part, out_ref in enumerate(outs):
        rows = slice(part * piece, (part + 1) * piece)
        out_ref[:, :body] = body_ref[rows, :]
        for index, block in enumerate(blocks):
            out_ref[:, body + index * LANES : body + (index + 1) * LANES] = block[rows]


def add_bf16(a, b):
    return (a.astype(jnp.float32) + b.astype(jnp.float32)).astype(jnp.bfloat16)


def merge_kernel(keep_ref, recv_ref, *outs):
    piece = outs[0].shape[0]
    for part, out_ref in enumerate(outs):
        rows = slice(part * piece, (part + 1) * piece)
        out_ref[...] = add_bf16(keep_ref[rows, :], recv_ref[rows, :])


def final_kernel(keep_ref, recv_ref, out_ref):
    out_ref[...] = add_bf16(keep_ref[...], recv_ref[...])


def call(kernel, outs, *args, scratch=(), limit=16 << 20, space=None):
    specs = {} if space is None else {"in_specs": [pl.BlockSpec(memory_space=space)] * len(args)}
    if space is not None:
        args = [pltpu.with_memory_space_constraint(arg, space) for arg in args]
    return pl.pallas_call(
        kernel,
        out_shape=outs,
        **specs,
        scratch_shapes=list(scratch),
        compiler_params=pltpu.CompilerParams(vmem_limit_bytes=limit),
    )(*args)


def plane_of(*shape):
    return jax.ShapeDtypeStruct(shape, jnp.bfloat16)


def shards(spectra, tap_offsets, tap_weights, trial_map, delays):
    band, seg = spectra.shape
    trials = trial_map.shape[1]
    freq_count = lax.axis_size("freq")
    tm_count = lax.axis_size("tm")
    levels = freq_count.bit_length() - 1
    rows = trials // 2
    span = levels * SHIFT
    tail = -(-(MAXOFF - 1 + span) // LANES) * LANES
    body = seg - tail

    def scratch(columns):
        leaf_rows = columns + span
        lhs_rows = leaf_rows + FINE * (PLANES - 1)
        return (
            pltpu.VMEM((lhs_rows + FINE, LANES), jnp.float32),
            pltpu.VMEM((lhs_rows, FINE * band), jnp.bfloat16),
            pltpu.VMEM((lhs_rows, PLANES * rows), jnp.float32),
            pltpu.VMEM((leaf_rows, rows), jnp.float32),
        )

    edge, samples, lags, weights, chosen, lateness = call(
        load_kernel,
        [
            plane_of(band, tail),
            plane_of(band, seg),
            jax.ShapeDtypeStruct((band, trials), jnp.int32),
            plane_of(band, trials),
            jax.ShapeDtypeStruct((1, trials), jnp.int32),
            jax.ShapeDtypeStruct(delays.shape, jnp.int32),
        ],
        spectra,
        jnp.swapaxes(tap_offsets[0], 0, 1),
        jnp.swapaxes(tap_weights[0], 0, 1),
        trial_map,
        delays,
        scratch=(pltpu.SemaphoreType.DMA((6,)),),
        space=pltpu.HBM,
    )
    ring = [((m + 1) % tm_count, m) for m in range(tm_count)]
    following = lax.ppermute(edge, "tm", ring)
    planes, taps, columns = call(
        functools.partial(main_kernel, freq_count),
        [
            plane_of(rows, body),
            plane_of(FINE * band, PLANES * rows),
            jax.ShapeDtypeStruct((8, rows), jnp.int32),
        ],
        samples,
        lags,
        weights,
        chosen,
        lateness,
        scratch=scratch(body),
    )
    parts = 4 if levels > 1 else 2
    pieces = call(
        functools.partial(tail_kernel, freq_count, tm_count, parts),
        [plane_of(rows // parts, seg)] * parts,
        samples,
        following,
        taps,
        columns,
        planes,
        scratch=scratch(tail),
    )
    for level in range(levels - 1):
        swap = [(i, i ^ (1 << level)) for i in range(freq_count)]
        keep_first, keep_next, send_first, send_next = pieces
        count = 1 if level == levels - 2 else 2
        shapes = [plane_of(keep_first.shape[0] // count, seg)] * count
        early = lax.ppermute(send_next, "freq", swap)
        late = lax.ppermute(send_first, "freq", swap)
        forwarded = call(merge_kernel, shapes, keep_next, early)
        kept = call(merge_kernel, shapes, keep_first, late)
        pieces = [*kept, *forwarded]
    keep, send = pieces
    recv = lax.ppermute(send, "freq", [(i, i ^ (1 << (levels - 1))) for i in range(freq_count)])
    return call(final_kernel, plane_of(*keep.shape), keep, recv)


def solution(mesh):
    return jax.shard_map(
        shards,
        mesh=mesh,
        in_specs=(
            P(("beam", "freq"), "tm"),
            P("freq", None, None),
            P("freq", None, None),
            P("freq", None),
            P(),
        ),
        out_specs=P(("beam", "freq", "trial"), "tm"),
        check_vma=False,
    )
```

```python
import functools

import jax
import jax.numpy as jnp
from jax import lax
from jax.experimental import pallas as pl
from jax.experimental.pallas import tpu as pltpu
from jax.sharding import PartitionSpec as P

MAXOFF = 32
SHIFT = 32
LANES = 128
FINE = 8
PLANES = (MAXOFF - 1 + FINE - 1) // FINE + 1


def own_columns(freq_count, map_ref, del_ref):
    trials = map_ref.shape[1]
    core_count = lax.axis_size("trial")
    row_block = trials // (core_count * freq_count)
    rows = trials // core_count
    levels = freq_count.bit_length() - 1
    freq_index = lax.axis_index("freq")
    core_index = lax.axis_index("trial")
    total = jnp.zeros((1, trials), jnp.int32)
    for level in range(levels):
        node = freq_count - (freq_count >> level) + lax.shift_right_logical(freq_index, level + 1)
        bit = lax.shift_right_logical(freq_index, level) & 1
        total = total + del_ref[pl.ds(node, 1), :] * bit
    first = lax.broadcasted_iota(jnp.int32, (8, trials), 0) == 0
    both = jnp.where(
        first, jnp.broadcast_to(map_ref[...], (8, trials)), jnp.broadcast_to(total, (8, trials))
    )
    place = lax.broadcasted_iota(jnp.int32, (8, rows), 1) // row_block
    mine = jnp.zeros((8, rows), jnp.int32)
    for r in range(freq_count):
        core = core_index if r == 0 else core_count - 1 - core_index
        start = ((freq_index ^ r) * core_count + core) * row_block
        turn = lax.rem(r * row_block - start + trials, trials)
        mine = jnp.where(place == r, pltpu.roll(both, turn, 1)[:, :rows], mine)
    return mine


def build_taps(off_ref, wt_ref, mine, rhs_ref):
    band, trials = wt_ref.shape
    rows = mine.shape[1]
    picker = mine[0:1, :] == lax.broadcasted_iota(jnp.int32, (trials, rows), 0)
    picker = picker.astype(jnp.float32).astype(jnp.bfloat16)
    tables = jnp.concatenate([wt_ref[...], off_ref[...].astype(jnp.float32).astype(jnp.bfloat16)], axis=0)
    picked = jnp.dot(tables, picker, preferred_element_type=jnp.float32)
    weights = picked[:band]
    lags = picked[band:].astype(jnp.int32) + (mine[1:2, :] & (FINE - 1))
    for fine in range(FINE):
        for plane in range(PLANES):
            rhs_ref[fine * band : (fine + 1) * band, plane * rows : (plane + 1) * rows] = jnp.where(
                lags == plane * FINE + fine, weights, 0.0
            ).astype(jnp.bfloat16)


def convolve(window, span, columns, delay_row, rhs_ref, time_ref, lhs_ref, plane_ref, leaf_ref):
    band = window.shape[0]
    rows = delay_row.shape[1]
    leaf_rows = columns + span
    lhs_rows = leaf_rows + FINE * (PLANES - 1)
    time_rows = lhs_rows + FINE
    turned = jnp.transpose(jnp.concatenate([window] * (LANES // band), axis=0).astype(jnp.float32))
    time_ref[:time_rows, :] = turned[:time_rows, :]
    low_lanes = lax.broadcasted_iota(jnp.int32, (lhs_rows, LANES), 1) < band
    for pair in range(FINE // 2):
        lhs_ref[:lhs_rows, pair * LANES : (pair + 1) * LANES] = jnp.where(
            low_lanes,
            time_ref[2 * pair : 2 * pair + lhs_rows, :],
            time_ref[2 * pair + 1 : 2 * pair + 1 + lhs_rows, :],
        ).astype(jnp.bfloat16)
    plane_ref[:lhs_rows, :] = jnp.dot(lhs_ref[:lhs_rows, :], rhs_ref[...], preferred_element_type=jnp.float32)
    leaf = plane_ref[:leaf_rows, :rows]
    for plane in range(1, PLANES):
        leaf = leaf + plane_ref[plane * FINE : plane * FINE + leaf_rows, plane * rows : (plane + 1) * rows]
    leaf_ref[:leaf_rows, :] = leaf
    steps = [FINE]
    while steps[-1] * 2 <= span:
        steps.append(steps[-1] * 2)
    blocks = []
    for start in range(0, columns, LANES):
        part = leaf_ref[start : start + LANES + span, :]
        for step in reversed(steps):
            length = LANES + sum(s for s in steps if s < step)
            length = min(length, part.shape[0])
            take = jnp.broadcast_to((delay_row & step) != 0, (length, rows))
            moved = part[step : step + length]
            if moved.shape[0] < length:
                moved = jnp.concatenate([moved, jnp.zeros((length - moved.shape[0], rows), jnp.float32)], axis=0)
            part = jnp.where(take, moved, part[:length])
        blocks.append(jnp.transpose(part[:LANES]).astype(jnp.bfloat16))
    return blocks


def load_kernel(x_hbm, off_hbm, wt_hbm, map_hbm, del_hbm, edge_ref, x_ref, off_ref, wt_ref, map_ref, del_ref, sems):
    moves = [
        pltpu.make_async_copy(source, target, sems.at[index])
        for index, (source, target) in enumerate(
            (
                (x_hbm.at[:, : edge_ref.shape[1]], edge_ref),
                (x_hbm, x_ref),
                (off_hbm, off_ref),
                (wt_hbm, wt_ref),
                (map_hbm, map_ref),
                (del_hbm, del_ref),
            )
        )
    ]
    for move in moves:
        move.start()
    for move in moves:
        move.wait()


def main_kernel(
    freq_count, x_ref, off_ref, wt_ref, map_ref, del_ref,
    body_ref, rhs_ref, delay_ref, time_ref, lhs_ref, plane_ref, leaf_ref,
):
    mine = own_columns(freq_count, map_ref, del_ref)
    build_taps(off_ref, wt_ref, mine, rhs_ref)
    delay_ref[...] = mine
    columns = body_ref.shape[1]
    span = (freq_count.bit_length() - 1) * SHIFT
    blocks = convolve(x_ref[...], span, columns, mine[1:2, :], rhs_ref, time_ref, lhs_ref, plane_ref, leaf_ref)
    for index, block in enumerate(blocks):
        body_ref[:, index * LANES : (index + 1) * LANES] = block


def tail_kernel(
    freq_count, tm_count, parts, x_ref, next_ref, rhs_ref, delay_ref, body_ref, *rest
):
    outs, (time_ref, lhs_ref, plane_ref, leaf_ref) = rest[:parts], rest[parts:]
    body = body_ref.shape[1]
    tail = x_ref.shape[1] - body
    piece = outs[0].shape[0]
    span = (freq_count.bit_length() - 1) * SHIFT
    inside = lax.axis_index("tm") < tm_count - 1
    following = jnp.where(inside, next_ref[...].astype(jnp.float32), 0.0).astype(jnp.bfloat16)
    window = jnp.concatenate([x_ref[:, body:], following], axis=1)
    blocks = convolve(window, span, tail, delay_ref[1:2, :], rhs_ref, time_ref, lhs_ref, plane_ref, leaf_ref)
    for part, out_ref in enumerate(outs):
        rows = slice(part * piece, (part + 1) * piece)
        out_ref[:, :body] = body_ref[rows, :]
        for index, block in enumerate(blocks):
            out_ref[:, body + index * LANES : body + (index + 1) * LANES] = block[rows]


def add_bf16(a, b):
    return (a.astype(jnp.float32) + b.astype(jnp.float32)).astype(jnp.bfloat16)


def final_kernel(order, *refs):
    planes = [refs[order.index(r)][...] for r in range(len(order))]
    while len(planes) > 1:
        planes = [add_bf16(lower, upper) for lower, upper in zip(planes[::2], planes[1::2])]
    refs[-1][...] = planes[0]


def call(kernel, outs, *args, scratch=(), limit=16 << 20, space=None):
    specs = {} if space is None else {"in_specs": [pl.BlockSpec(memory_space=space)] * len(args)}
    if space is not None:
        args = [pltpu.with_memory_space_constraint(arg, space) for arg in args]
    return pl.pallas_call(
        kernel,
        out_shape=outs,
        **specs,
        scratch_shapes=list(scratch),
        compiler_params=pltpu.CompilerParams(vmem_limit_bytes=limit),
    )(*args)


def plane_of(*shape):
    return jax.ShapeDtypeStruct(shape, jnp.bfloat16)


def shards(spectra, tap_offsets, tap_weights, trial_map, delays):
    band, seg = spectra.shape
    trials = trial_map.shape[1]
    freq_count = lax.axis_size("freq")
    tm_count = lax.axis_size("tm")
    levels = freq_count.bit_length() - 1
    core_count = lax.axis_size("trial")
    rows = trials // core_count
    span = levels * SHIFT
    tail = -(-(MAXOFF - 1 + span) // LANES) * LANES
    body = seg - tail

    def scratch(columns):
        leaf_rows = columns + span
        lhs_rows = leaf_rows + FINE * (PLANES - 1)
        return (
            pltpu.VMEM((lhs_rows + FINE, LANES), jnp.float32),
            pltpu.VMEM((lhs_rows, FINE * band), jnp.bfloat16),
            pltpu.VMEM((lhs_rows, PLANES * rows), jnp.float32),
            pltpu.VMEM((leaf_rows, rows), jnp.float32),
        )

    edge, samples, lags, weights, chosen, lateness = call(
        load_kernel,
        [
            plane_of(band, tail),
            plane_of(band, seg),
            jax.ShapeDtypeStruct((band, trials), jnp.int32),
            plane_of(band, trials),
            jax.ShapeDtypeStruct((1, trials), jnp.int32),
            jax.ShapeDtypeStruct(delays.shape, jnp.int32),
        ],
        spectra,
        jnp.swapaxes(tap_offsets[0], 0, 1),
        jnp.swapaxes(tap_weights[0], 0, 1),
        trial_map,
        delays,
        scratch=(pltpu.SemaphoreType.DMA((6,)),),
        space=pltpu.HBM,
    )
    ring = [
        (((m + 1) % tm_count) * core_count + core_count - 1 - c, m * core_count + c)
        for m in range(tm_count)
        for c in range(core_count)
    ]
    following = lax.ppermute(edge, ("tm", "trial"), ring)
    planes, taps, columns = call(
        functools.partial(main_kernel, freq_count),
        [
            plane_of(rows, body),
            plane_of(FINE * band, PLANES * rows),
            jax.ShapeDtypeStruct((8, rows), jnp.int32),
        ],
        samples,
        lags,
        weights,
        chosen,
        lateness,
        scratch=scratch(body),
    )
    blocks = call(
        functools.partial(tail_kernel, freq_count, tm_count, freq_count),
        [plane_of(rows // freq_count, seg)] * freq_count,
        samples,
        following,
        taps,
        columns,
        planes,
        scratch=scratch(tail),
    )
    order = [0, freq_count - 1, *range(1, freq_count - 1)]
    received = [blocks[0]]
    for r in order[1:]:
        route = [
            (f * core_count + c, (f ^ r) * core_count + core_count - 1 - c)
            for f in range(freq_count)
            for c in range(core_count)
        ]
        received.append(lax.ppermute(blocks[r], ("freq", "trial"), route))
    return call(functools.partial(final_kernel, order), plane_of(*blocks[0].shape), *received)


def solution(mesh):
    return jax.shard_map(
        shards,
        mesh=mesh,
        in_specs=(
            P(("beam", "freq"), "tm"),
            P("freq", None, None),
            P("freq", None, None),
            P("freq", None),
            P(),
        ),
        out_specs=P(("beam", "freq", "trial"), "tm"),
        check_vma=False,
    )
```

```python
import functools

import jax
import jax.numpy as jnp
from jax import lax
from jax.experimental import pallas as pl
from jax.experimental.pallas import tpu as pltpu
from jax.sharding import PartitionSpec as P

MAXOFF = 32
SHIFT = 32
LANES = 128
FINE = 8
PLANES = (MAXOFF - 1 + FINE - 1) // FINE + 1


def shared_pairs(freq_count):
    return [(r, r + 1) for r in range(1, freq_count - 1, 2)]


def block_order(freq_count, core_index):
    other = 1 - core_index
    order = [(0, core_index)]
    for first, second in shared_pairs(freq_count):
        mine = first + core_index * (second - first)
        order += [(mine, core_index), (mine, other)]
    return [*order, (freq_count - 1, other)]


def own_columns(freq_count, map_ref, del_ref):
    trials = map_ref.shape[1]
    core_count = lax.axis_size("trial")
    row_block = trials // (core_count * freq_count)
    rows = trials // core_count
    levels = freq_count.bit_length() - 1
    freq_index = lax.axis_index("freq")
    core_index = lax.axis_index("trial")
    total = jnp.zeros((1, trials), jnp.int32)
    for level in range(levels):
        node = freq_count - (freq_count >> level) + lax.shift_right_logical(freq_index, level + 1)
        bit = lax.shift_right_logical(freq_index, level) & 1
        total = total + del_ref[pl.ds(node, 1), :] * bit
    first = lax.broadcasted_iota(jnp.int32, (8, trials), 0) == 0
    both = jnp.where(
        first, jnp.broadcast_to(map_ref[...], (8, trials)), jnp.broadcast_to(total, (8, trials))
    )
    place = lax.broadcasted_iota(jnp.int32, (8, rows), 1) // row_block
    mine = jnp.zeros((8, rows), jnp.int32)
    for position, (distance, core) in enumerate(block_order(freq_count, core_index)):
        start = ((freq_index ^ distance) * core_count + core) * row_block
        turn = lax.rem(position * row_block - start + trials, trials)
        mine = jnp.where(place == position, pltpu.roll(both, turn, 1)[:, :rows], mine)
    return mine


def build_taps(off_ref, wt_ref, mine, rhs_ref):
    band, trials = wt_ref.shape
    rows = mine.shape[1]
    picker = mine[0:1, :] == lax.broadcasted_iota(jnp.int32, (trials, rows), 0)
    picker = picker.astype(jnp.float32).astype(jnp.bfloat16)
    tables = jnp.concatenate([wt_ref[...], off_ref[...].astype(jnp.float32).astype(jnp.bfloat16)], axis=0)
    picked = jnp.dot(tables, picker, preferred_element_type=jnp.float32)
    weights = picked[:band]
    lags = picked[band:].astype(jnp.int32) + (mine[1:2, :] & (FINE - 1))
    for fine in range(FINE):
        for plane in range(PLANES):
            rhs_ref[fine * band : (fine + 1) * band, plane * rows : (plane + 1) * rows] = jnp.where(
                lags == plane * FINE + fine, weights, 0.0
            ).astype(jnp.bfloat16)


def convolve(window, span, columns, delay_row, rhs_ref, time_ref, lhs_ref, plane_ref, leaf_ref):
    band = window.shape[0]
    rows = delay_row.shape[1]
    leaf_rows = columns + span
    lhs_rows = leaf_rows + FINE * (PLANES - 1)
    time_rows = lhs_rows + FINE
    turned = jnp.transpose(jnp.concatenate([window] * (LANES // band), axis=0).astype(jnp.float32))
    time_ref[:time_rows, :] = turned[:time_rows, :]
    low_lanes = lax.broadcasted_iota(jnp.int32, (lhs_rows, LANES), 1) < band
    for pair in range(FINE // 2):
        lhs_ref[:lhs_rows, pair * LANES : (pair + 1) * LANES] = jnp.where(
            low_lanes,
            time_ref[2 * pair : 2 * pair + lhs_rows, :],
            time_ref[2 * pair + 1 : 2 * pair + 1 + lhs_rows, :],
        ).astype(jnp.bfloat16)
    plane_ref[:lhs_rows, :] = jnp.dot(lhs_ref[:lhs_rows, :], rhs_ref[...], preferred_element_type=jnp.float32)
    leaf = plane_ref[:leaf_rows, :rows]
    for plane in range(1, PLANES):
        leaf = leaf + plane_ref[plane * FINE : plane * FINE + leaf_rows, plane * rows : (plane + 1) * rows]
    leaf_ref[:leaf_rows, :] = leaf
    steps = [FINE]
    while steps[-1] * 2 <= span:
        steps.append(steps[-1] * 2)
    blocks = []
    for start in range(0, columns, LANES):
        part = leaf_ref[start : start + LANES + span, :]
        for step in reversed(steps):
            length = LANES + sum(s for s in steps if s < step)
            length = min(length, part.shape[0])
            take = jnp.broadcast_to((delay_row & step) != 0, (length, rows))
            moved = part[step : step + length]
            if moved.shape[0] < length:
                moved = jnp.concatenate([moved, jnp.zeros((length - moved.shape[0], rows), jnp.float32)], axis=0)
            part = jnp.where(take, moved, part[:length])
        blocks.append(jnp.transpose(part[:LANES]).astype(jnp.bfloat16))
    return blocks


def load_kernel(x_hbm, off_hbm, wt_hbm, map_hbm, del_hbm, edge_ref, x_ref, off_ref, wt_ref, map_ref, del_ref, sems):
    moves = [
        pltpu.make_async_copy(source, target, sems.at[index])
        for index, (source, target) in enumerate(
            (
                (x_hbm.at[:, : edge_ref.shape[1]], edge_ref),
                (x_hbm, x_ref),
                (off_hbm, off_ref),
                (wt_hbm, wt_ref),
                (map_hbm, map_ref),
                (del_hbm, del_ref),
            )
        )
    ]
    for move in moves:
        move.start()
    for move in moves:
        move.wait()


def main_kernel(
    freq_count, x_ref, off_ref, wt_ref, map_ref, del_ref,
    body_ref, rhs_ref, delay_ref, time_ref, lhs_ref, plane_ref, leaf_ref,
):
    mine = own_columns(freq_count, map_ref, del_ref)
    build_taps(off_ref, wt_ref, mine, rhs_ref)
    delay_ref[...] = mine
    columns = body_ref.shape[1]
    span = (freq_count.bit_length() - 1) * SHIFT
    blocks = convolve(x_ref[...], span, columns, mine[1:2, :], rhs_ref, time_ref, lhs_ref, plane_ref, leaf_ref)
    for index, block in enumerate(blocks):
        body_ref[:, index * LANES : (index + 1) * LANES] = block


def tail_kernel(
    freq_count, tm_count, x_ref, next_ref, rhs_ref, delay_ref, body_ref, *rest
):
    outs, (time_ref, lhs_ref, plane_ref, leaf_ref) = rest[:-4], rest[-4:]
    body = body_ref.shape[1]
    tail = x_ref.shape[1] - body
    span = (freq_count.bit_length() - 1) * SHIFT
    inside = lax.axis_index("tm") < tm_count - 1
    following = jnp.where(inside, next_ref[...].astype(jnp.float32), 0.0).astype(jnp.bfloat16)
    window = jnp.concatenate([x_ref[:, body:], following], axis=1)
    blocks = convolve(window, span, tail, delay_ref[1:2, :], rhs_ref, time_ref, lhs_ref, plane_ref, leaf_ref)
    first = 0
    for out_ref in outs:
        rows = slice(first, first + out_ref.shape[0])
        first += out_ref.shape[0]
        out_ref[:, :body] = body_ref[rows, :]
        for index, block in enumerate(blocks):
            out_ref[:, body + index * LANES : body + (index + 1) * LANES] = block[rows]


def second_half_kernel(both_ref, out_ref):
    out_ref[...] = both_ref[out_ref.shape[0] :, :]


def final_kernel(freq_count, own_ref, *refs):
    piece = own_ref.shape[0]
    first_core = lax.axis_index("trial") == 0
    planes = [own_ref[...].astype(jnp.float32)]
    for pair in range(len(shared_pairs(freq_count))):
        here = refs[2 * pair][:piece, :].astype(jnp.float32)
        there = refs[2 * pair + 1][...].astype(jnp.float32)
        planes += [jnp.where(first_core, here, there), jnp.where(first_core, there, here)]
    planes.append(refs[-2][...].astype(jnp.float32))
    while len(planes) > 1:
        planes = [
            (lower + upper).astype(jnp.bfloat16).astype(jnp.float32) for lower, upper in zip(planes[::2], planes[1::2])
        ]
    refs[-1][...] = planes[0].astype(jnp.bfloat16)


def call(kernel, outs, *args, scratch=(), limit=16 << 20, space=None):
    specs = {} if space is None else {"in_specs": [pl.BlockSpec(memory_space=space)] * len(args)}
    if space is not None:
        args = [pltpu.with_memory_space_constraint(arg, space) for arg in args]
    return pl.pallas_call(
        kernel,
        out_shape=outs,
        **specs,
        scratch_shapes=list(scratch),
        compiler_params=pltpu.CompilerParams(vmem_limit_bytes=limit),
    )(*args)


def plane_of(*shape):
    return jax.ShapeDtypeStruct(shape, jnp.bfloat16)


def shards(spectra, tap_offsets, tap_weights, trial_map, delays):
    band, seg = spectra.shape
    trials = trial_map.shape[1]
    freq_count = lax.axis_size("freq")
    tm_count = lax.axis_size("tm")
    levels = freq_count.bit_length() - 1
    core_count = lax.axis_size("trial")
    rows = trials // core_count
    span = levels * SHIFT
    tail = -(-(MAXOFF - 1 + span) // LANES) * LANES
    body = seg - tail

    def scratch(columns):
        leaf_rows = columns + span
        lhs_rows = leaf_rows + FINE * (PLANES - 1)
        return (
            pltpu.VMEM((lhs_rows + FINE, LANES), jnp.float32),
            pltpu.VMEM((lhs_rows, FINE * band), jnp.bfloat16),
            pltpu.VMEM((lhs_rows, PLANES * rows), jnp.float32),
            pltpu.VMEM((leaf_rows, rows), jnp.float32),
        )

    edge, samples, lags, weights, chosen, lateness = call(
        load_kernel,
        [
            plane_of(band, tail),
            plane_of(band, seg),
            jax.ShapeDtypeStruct((band, trials), jnp.int32),
            plane_of(band, trials),
            jax.ShapeDtypeStruct((1, trials), jnp.int32),
            jax.ShapeDtypeStruct(delays.shape, jnp.int32),
        ],
        spectra,
        jnp.swapaxes(tap_offsets[0], 0, 1),
        jnp.swapaxes(tap_weights[0], 0, 1),
        trial_map,
        delays,
        scratch=(pltpu.SemaphoreType.DMA((6,)),),
        space=pltpu.HBM,
    )
    ring = [
        (((m + 1) % tm_count) * core_count + core_count - 1 - c, m * core_count + c)
        for m in range(tm_count)
        for c in range(core_count)
    ]
    following = lax.ppermute(edge, ("tm", "trial"), ring)
    planes, taps, columns = call(
        functools.partial(main_kernel, freq_count),
        [
            plane_of(rows, body),
            plane_of(FINE * band, PLANES * rows),
            jax.ShapeDtypeStruct((8, rows), jnp.int32),
        ],
        samples,
        lags,
        weights,
        chosen,
        lateness,
        scratch=scratch(body),
    )
    piece = rows // freq_count
    pairs = shared_pairs(freq_count)
    own, *shared, far = call(
        functools.partial(tail_kernel, freq_count, tm_count),
        [plane_of(piece, seg), *[plane_of(2 * piece, seg)] * len(pairs), plane_of(piece, seg)],
        samples,
        following,
        taps,
        columns,
        planes,
        scratch=scratch(tail),
    )
    devices = [(f, c) for f in range(freq_count) for c in range(core_count)]
    arrived = []
    for pair, block in zip(pairs, shared):
        route = [(f * core_count + c, (f ^ pair[c]) * core_count + c) for f, c in devices]
        arrived.append(lax.ppermute(block, ("freq", "trial"), route))
    route = [(f * core_count + c, (f ^ (freq_count - 1)) * core_count + core_count - 1 - c) for f, c in devices]
    far = lax.ppermute(far, ("freq", "trial"), route)
    received = []
    for both in arrived:
        handed = call(second_half_kernel, plane_of(piece, seg), both)
        received += [both, lax.ppermute(handed, "trial", [(0, 1), (1, 0)])]
    return call(functools.partial(final_kernel, freq_count), plane_of(piece, seg), own, *received, far)


def solution(mesh):
    return jax.shard_map(
        shards,
        mesh=mesh,
        in_specs=(
            P(("beam", "freq"), "tm"),
            P("freq", None, None),
            P("freq", None, None),
            P("freq", None),
            P(),
        ),
        out_specs=P(("beam", "freq", "trial"), "tm"),
        check_vma=False,
    )
```

```python
import functools

import jax
import jax.numpy as jnp
from jax import lax
from jax.experimental import pallas as pl
from jax.experimental.pallas import tpu as pltpu
from jax.sharding import PartitionSpec as P


MAXOFF = 32
SHIFT = 32
LANES = 128
FINE = 8
PLANES = (MAXOFF - 1 + FINE - 1) // FINE + 1


def shared_pairs(freq_count):
    return [(r, r + 1) for r in range(1, freq_count - 1, 2)]


def block_order(freq_count, core_index):
    other = 1 - core_index
    order = [(0, core_index)]
    for first, second in shared_pairs(freq_count):
        mine = first + core_index * (second - first)
        order += [(mine, core_index), (mine, other)]
    return [*order, (freq_count - 1, other)]


def own_columns(freq_count, map_ref, del_ref):
    trials = map_ref.shape[1]
    core_count = lax.axis_size("trial")
    row_block = trials // (core_count * freq_count)
    rows = trials // core_count
    levels = freq_count.bit_length() - 1
    freq_index = lax.axis_index("freq")
    core_index = lax.axis_index("trial")
    total = jnp.zeros((1, trials), jnp.int32)
    for level in range(levels):
        node = freq_count - (freq_count >> level) + lax.shift_right_logical(freq_index, level + 1)
        bit = lax.shift_right_logical(freq_index, level) & 1
        total = total + del_ref[pl.ds(node, 1), :] * bit
    first = lax.broadcasted_iota(jnp.int32, (8, trials), 0) == 0
    both = jnp.where(
        first, jnp.broadcast_to(map_ref[...], (8, trials)), jnp.broadcast_to(total, (8, trials))
    )
    place = lax.broadcasted_iota(jnp.int32, (8, rows), 1) // row_block
    mine = jnp.zeros((8, rows), jnp.int32)
    for position, (distance, core) in enumerate(block_order(freq_count, core_index)):
        start = ((freq_index ^ distance) * core_count + core) * row_block
        turn = lax.rem(position * row_block - start + trials, trials)
        mine = jnp.where(place == position, pltpu.roll(both, turn, 1)[:, :rows], mine)
    return mine


def build_taps(off_ref, wt_ref, mine, rhs_ref):
    band, trials = wt_ref.shape
    rows = mine.shape[1]
    picker = mine[0:1, :] == lax.broadcasted_iota(jnp.int32, (trials, rows), 0)
    picker = picker.astype(jnp.float32).astype(jnp.bfloat16)
    tables = jnp.concatenate([wt_ref[...], off_ref[...].astype(jnp.float32).astype(jnp.bfloat16)], axis=0)
    picked = jnp.dot(tables, picker, preferred_element_type=jnp.float32)
    weights = picked[:band]
    lags = picked[band:].astype(jnp.int32) + (mine[1:2, :] & (FINE - 1))
    for fine in range(FINE):
        for plane in range(PLANES):
            rhs_ref[fine * band : (fine + 1) * band, plane * rows : (plane + 1) * rows] = jnp.where(
                lags == plane * FINE + fine, weights, 0.0
            ).astype(jnp.bfloat16)


def convolve(window, span, columns, delay_row, rhs_ref, time_ref, lhs_ref, plane_ref, leaf_ref):
    band = window.shape[0]
    rows = delay_row.shape[1]
    leaf_rows = columns + span
    lhs_rows = leaf_rows + FINE * (PLANES - 1)
    time_rows = lhs_rows + FINE
    turned = jnp.transpose(jnp.concatenate([window] * (LANES // band), axis=0).astype(jnp.float32))
    time_ref[:time_rows, :] = turned[:time_rows, :]
    low_lanes = lax.broadcasted_iota(jnp.int32, (lhs_rows, LANES), 1) < band
    for pair in range(FINE // 2):
        lhs_ref[:lhs_rows, pair * LANES : (pair + 1) * LANES] = jnp.where(
            low_lanes,
            time_ref[2 * pair : 2 * pair + lhs_rows, :],
            time_ref[2 * pair + 1 : 2 * pair + 1 + lhs_rows, :],
        ).astype(jnp.bfloat16)
    plane_ref[:lhs_rows, :] = jnp.dot(lhs_ref[:lhs_rows, :], rhs_ref[...], preferred_element_type=jnp.float32)
    leaf = plane_ref[:leaf_rows, :rows]
    for plane in range(1, PLANES):
        leaf = leaf + plane_ref[plane * FINE : plane * FINE + leaf_rows, plane * rows : (plane + 1) * rows]
    leaf_ref[:leaf_rows, :] = leaf
    steps = [FINE]
    while steps[-1] * 2 <= span:
        steps.append(steps[-1] * 2)
    blocks = []
    for start in range(0, columns, LANES):
        part = leaf_ref[start : start + LANES + span, :]
        for step in reversed(steps):
            length = LANES + sum(s for s in steps if s < step)
            length = min(length, part.shape[0])
            take = jnp.broadcast_to((delay_row & step) != 0, (length, rows))
            moved = part[step : step + length]
            if moved.shape[0] < length:
                moved = jnp.concatenate([moved, jnp.zeros((length - moved.shape[0], rows), jnp.float32)], axis=0)
            part = jnp.where(take, moved, part[:length])
        blocks.append(jnp.transpose(part[:LANES]).astype(jnp.bfloat16))
    return blocks


def store_rows(blocks, outs):
    first = 0
    for out_ref in outs:
        rows = slice(first, first + out_ref.shape[0])
        first += out_ref.shape[0]
        for index, block in enumerate(blocks):
            out_ref[:, index * LANES : (index + 1) * LANES] = block[rows]


def load_kernel(x_hbm, off_hbm, wt_hbm, map_hbm, del_hbm, edge_ref, x_ref, off_ref, wt_ref, map_ref, del_ref, sems):
    moves = [
        pltpu.make_async_copy(source, target, sems.at[index])
        for index, (source, target) in enumerate(
            (
                (x_hbm, x_ref),
                (off_hbm, off_ref),
                (wt_hbm, wt_ref),
                (map_hbm, map_ref),
                (del_hbm, del_ref),
            )
        )
    ]
    for move in moves:
        move.start()
    moves[0].wait()
    edge_ref[...] = x_ref[:, : edge_ref.shape[1]]
    for move in moves[1:]:
        move.wait()


def main_kernel(
    freq_count, x_ref, off_ref, wt_ref, map_ref, del_ref, rhs_ref, delay_ref, *rest
):
    outs, (time_ref, lhs_ref, plane_ref, leaf_ref) = rest[:-4], rest[-4:]
    mine = own_columns(freq_count, map_ref, del_ref)
    build_taps(off_ref, wt_ref, mine, rhs_ref)
    delay_ref[...] = mine
    columns = outs[0].shape[1]
    span = (freq_count.bit_length() - 1) * SHIFT
    blocks = convolve(x_ref[...], span, columns, mine[1:2, :], rhs_ref, time_ref, lhs_ref, plane_ref, leaf_ref)
    store_rows(blocks, outs)


def tail_kernel(freq_count, tm_count, x_ref, next_ref, rhs_ref, delay_ref, far_body_ref, *rest):
    outs, far_ref, (time_ref, lhs_ref, plane_ref, leaf_ref) = rest[:-5], rest[-5], rest[-4:]
    tail = outs[0].shape[1]
    body = x_ref.shape[1] - tail
    span = (freq_count.bit_length() - 1) * SHIFT
    inside = lax.axis_index("tm") < tm_count - 1
    following = jnp.where(inside, next_ref[...].astype(jnp.float32), 0.0).astype(jnp.bfloat16)
    window = jnp.concatenate([x_ref[:, body:], following], axis=1)
    blocks = convolve(window, span, tail, delay_ref[1:2, :], rhs_ref, time_ref, lhs_ref, plane_ref, leaf_ref)
    far_ref[:, :body] = far_body_ref[...]
    store_rows(blocks, [*outs, far_ref.at[:, body:]])


def second_half_kernel(body_ref, tail_ref, out_ref):
    piece, _ = out_ref.shape
    body = body_ref.shape[1]
    out_ref[:, :body] = body_ref[piece:, :]
    out_ref[:, body:] = tail_ref[piece:, :]


def final_kernel(freq_count, *refs):
    out_ref = refs[-1]
    piece, seg = out_ref.shape
    body = refs[0].shape[1]
    first_core = lax.axis_index("trial") == 0
    for part, columns in ((0, slice(0, body)), (1, slice(body, seg))):
        planes = [refs[part][...].astype(jnp.float32)]
        for pair in range(len(shared_pairs(freq_count))):
            here = refs[2 + 3 * pair + part][:piece, :].astype(jnp.float32)
            there = refs[2 + 3 * pair + 2][:, columns].astype(jnp.float32)
            planes += [jnp.where(first_core, here, there), jnp.where(first_core, there, here)]
        planes.append(refs[-2][:, columns].astype(jnp.float32))
        while len(planes) > 1:
            planes = [
                (lower + upper).astype(jnp.bfloat16).astype(jnp.float32)
                for lower, upper in zip(planes[::2], planes[1::2])
            ]
        out_ref[:, columns] = planes[0].astype(jnp.bfloat16)


def call(kernel, outs, *args, scratch=(), limit=16 << 20, space=None):
    specs = {} if space is None else {"in_specs": [pl.BlockSpec(memory_space=space)] * len(args)}
    if space is not None:
        args = [pltpu.with_memory_space_constraint(arg, space) for arg in args]
    return pl.pallas_call(
        kernel,
        out_shape=outs,
        **specs,
        scratch_shapes=list(scratch),
        compiler_params=pltpu.CompilerParams(vmem_limit_bytes=limit),
    )(*args)


def plane_of(*shape):
    return jax.ShapeDtypeStruct(shape, jnp.bfloat16)


def shards(spectra, tap_offsets, tap_weights, trial_map, delays):
    band, seg = spectra.shape
    trials = trial_map.shape[1]
    freq_count = lax.axis_size("freq")
    tm_count = lax.axis_size("tm")
    levels = freq_count.bit_length() - 1
    core_count = lax.axis_size("trial")
    rows = trials // core_count
    span = levels * SHIFT
    tail = -(-(MAXOFF - 1 + span) // LANES) * LANES
    body = seg - tail

    def scratch(columns):
        leaf_rows = columns + span
        lhs_rows = leaf_rows + FINE * (PLANES - 1)
        return (
            pltpu.VMEM((lhs_rows + FINE, LANES), jnp.float32),
            pltpu.VMEM((lhs_rows, FINE * band), jnp.bfloat16),
            pltpu.VMEM((lhs_rows, PLANES * rows), jnp.float32),
            pltpu.VMEM((leaf_rows, rows), jnp.float32),
        )

    edge, samples, lags, weights, chosen, lateness = call(
        load_kernel,
        [
            plane_of(band, tail),
            plane_of(band, seg),
            jax.ShapeDtypeStruct((band, trials), jnp.int32),
            plane_of(band, trials),
            jax.ShapeDtypeStruct((1, trials), jnp.int32),
            jax.ShapeDtypeStruct(delays.shape, jnp.int32),
        ],
        spectra,
        jnp.swapaxes(tap_offsets[0], 0, 1),
        jnp.swapaxes(tap_weights[0], 0, 1),
        trial_map,
        delays,
        scratch=(pltpu.SemaphoreType.DMA((5,)),),
        space=pltpu.HBM,
    )
    ring = [
        (((m + 1) % tm_count) * core_count + core_count - 1 - c, m * core_count + c)
        for m in range(tm_count)
        for c in range(core_count)
    ]
    following = lax.ppermute(edge, ("tm", "trial"), ring)
    piece = rows // freq_count
    pairs = shared_pairs(freq_count)
    heights = [piece, *[2 * piece] * len(pairs), piece]
    taps, columns, *bodies = call(
        functools.partial(main_kernel, freq_count),
        [
            plane_of(FINE * band, PLANES * rows),
            jax.ShapeDtypeStruct((8, rows), jnp.int32),
            *[plane_of(height, body) for height in heights],
        ],
        samples,
        lags,
        weights,
        chosen,
        lateness,
        scratch=scratch(body),
    )
    devices = [(f, c) for f in range(freq_count) for c in range(core_count)]

    def traded(blocks):
        arrived = []
        for pair, block in zip(pairs, blocks):
            route = [(f * core_count + c, (f ^ pair[c]) * core_count + c) for f, c in devices]
            arrived.append(lax.ppermute(block, ("freq", "trial"), route))
        return arrived

    own, *bodies, far_body = bodies
    bodies = traded(bodies)
    own_tail, *tails, far = call(
        functools.partial(tail_kernel, freq_count, tm_count),
        [*[plane_of(height, tail) for height in heights[:-1]], plane_of(piece, seg)],
        samples,
        following,
        taps,
        columns,
        far_body,
        scratch=scratch(tail),
    )
    tails = traded(tails)
    route = [(f * core_count + c, (f ^ (freq_count - 1)) * core_count + core_count - 1 - c) for f, c in devices]
    far = lax.ppermute(far, ("freq", "trial"), route)
    received = []
    for both in zip(bodies, tails):
        handed = call(second_half_kernel, plane_of(piece, seg), *both)
        received += [*both, lax.ppermute(handed, "trial", [(0, 1), (1, 0)])]
    return call(functools.partial(final_kernel, freq_count), plane_of(piece, seg), own, own_tail, *received, far)


def solution(mesh):
    return jax.shard_map(
        shards,
        mesh=mesh,
        in_specs=(
            P(("beam", "freq"), "tm"),
            P("freq", None, None),
            P("freq", None, None),
            P("freq", None),
            P(),
        ),
        out_specs=P(("beam", "freq", "trial"), "tm"),
        check_vma=False,
    )
```

```python
import functools

import jax
import jax.numpy as jnp
from jax import lax
from jax.experimental import pallas as pl
from jax.experimental.pallas import tpu as pltpu
from jax.sharding import PartitionSpec as P


MAXOFF = 32
SHIFT = 32
LANES = 128
FINE = 8
PLANES = (MAXOFF - 1 + FINE - 1) // FINE + 1


def shared_pairs(freq_count):
    return [(r, r + 1) for r in range(1, freq_count - 1, 2)]


def block_order(freq_count, core_index):
    other = 1 - core_index
    order = [(0, core_index)]
    for first, second in shared_pairs(freq_count):
        mine = first + core_index * (second - first)
        order += [(mine, core_index), (mine, other)]
    return [*order, (freq_count - 1, other)]


def own_columns(freq_count, map_ref, del_ref):
    trials = map_ref.shape[1]
    core_count = lax.axis_size("trial")
    row_block = trials // (core_count * freq_count)
    rows = trials // core_count
    levels = freq_count.bit_length() - 1
    freq_index = lax.axis_index("freq")
    core_index = lax.axis_index("trial")
    total = jnp.zeros((1, trials), jnp.int32)
    for level in range(levels):
        node = freq_count - (freq_count >> level) + lax.shift_right_logical(freq_index, level + 1)
        bit = lax.shift_right_logical(freq_index, level) & 1
        total = total + del_ref[pl.ds(node, 1), :] * bit
    first = lax.broadcasted_iota(jnp.int32, (8, trials), 0) == 0
    both = jnp.where(
        first, jnp.broadcast_to(map_ref[...], (8, trials)), jnp.broadcast_to(total, (8, trials))
    )
    place = lax.broadcasted_iota(jnp.int32, (8, rows), 1) // row_block
    mine = jnp.zeros((8, rows), jnp.int32)
    for position, (distance, core) in enumerate(block_order(freq_count, core_index)):
        start = ((freq_index ^ distance) * core_count + core) * row_block
        turn = lax.rem(position * row_block - start + trials, trials)
        mine = jnp.where(place == position, pltpu.roll(both, turn, 1)[:, :rows], mine)
    return mine


def build_taps(off_ref, wt_ref, mine, rhs_ref):
    band, trials = wt_ref.shape
    rows = mine.shape[1]
    picker = mine[0:1, :] == lax.broadcasted_iota(jnp.int32, (trials, rows), 0)
    picker = picker.astype(jnp.float32).astype(jnp.bfloat16)
    tables = jnp.concatenate([wt_ref[...], off_ref[...].astype(jnp.float32).astype(jnp.bfloat16)], axis=0)
    picked = jnp.dot(tables, picker, preferred_element_type=jnp.float32)
    weights = picked[:band]
    lags = picked[band:].astype(jnp.int32) + (mine[1:2, :] & (FINE - 1))
    for fine in range(FINE):
        for plane in range(PLANES):
            rhs_ref[fine * band : (fine + 1) * band, plane * rows : (plane + 1) * rows] = jnp.where(
                lags == plane * FINE + fine, weights, 0.0
            ).astype(jnp.bfloat16)


def convolve(window, span, columns, delay_row, rhs_ref, time_ref, lhs_ref, plane_ref, leaf_ref):
    band = window.shape[0]
    rows = delay_row.shape[1]
    leaf_rows = columns + span
    lhs_rows = leaf_rows + FINE * (PLANES - 1)
    time_rows = lhs_rows + FINE
    turned = jnp.transpose(jnp.concatenate([window] * (LANES // band), axis=0).astype(jnp.float32))
    time_ref[:time_rows, :] = turned[:time_rows, :]
    low_lanes = lax.broadcasted_iota(jnp.int32, (lhs_rows, LANES), 1) < band
    for pair in range(FINE // 2):
        lhs_ref[:lhs_rows, pair * LANES : (pair + 1) * LANES] = jnp.where(
            low_lanes,
            time_ref[2 * pair : 2 * pair + lhs_rows, :],
            time_ref[2 * pair + 1 : 2 * pair + 1 + lhs_rows, :],
        ).astype(jnp.bfloat16)
    plane_ref[:lhs_rows, :] = jnp.dot(lhs_ref[:lhs_rows, :], rhs_ref[...], preferred_element_type=jnp.float32)
    leaf = plane_ref[:leaf_rows, :rows]
    for plane in range(1, PLANES):
        leaf = leaf + plane_ref[plane * FINE : plane * FINE + leaf_rows, plane * rows : (plane + 1) * rows]
    leaf_ref[:leaf_rows, :] = leaf
    steps = [FINE]
    while steps[-1] * 2 <= span:
        steps.append(steps[-1] * 2)
    blocks = []
    for start in range(0, columns, LANES):
        part = leaf_ref[start : start + LANES + span, :]
        for step in reversed(steps):
            length = LANES + sum(s for s in steps if s < step)
            length = min(length, part.shape[0])
            take = jnp.broadcast_to((delay_row & step) != 0, (length, rows))
            moved = part[step : step + length]
            if moved.shape[0] < length:
                moved = jnp.concatenate([moved, jnp.zeros((length - moved.shape[0], rows), jnp.float32)], axis=0)
            part = jnp.where(take, moved, part[:length])
        blocks.append(jnp.transpose(part[:LANES]).astype(jnp.bfloat16))
    return blocks


def store_rows(blocks, outs):
    first = 0
    for out_ref in outs:
        rows = slice(first, first + out_ref.shape[0])
        first += out_ref.shape[0]
        for index, block in enumerate(blocks):
            out_ref[:, index * LANES : (index + 1) * LANES] = block[rows]


def load_kernel(
    freq_count, x_hbm, off_hbm, wt_hbm, map_hbm, del_hbm, edge_ref, x_ref, off_ref, wt_ref, mine_ref, map_ref, del_ref, sems
):
    targets = ((map_hbm, map_ref), (del_hbm, del_ref), (x_hbm, x_ref), (off_hbm, off_ref), (wt_hbm, wt_ref))
    moves = [pltpu.make_async_copy(source, target, sems.at[k]) for k, (source, target) in enumerate(targets)]
    for move in moves:
        move.start()
    for move in moves[:2]:
        move.wait()
    mine_ref[...] = own_columns(freq_count, map_ref, del_ref)
    moves[2].wait()
    edge_ref[...] = x_ref[:, : edge_ref.shape[1]]
    for move in moves[3:]:
        move.wait()


def main_kernel(
    freq_count, x_ref, off_ref, wt_ref, mine_ref, rhs_ref, *rest
):
    outs, (time_ref, lhs_ref, plane_ref, leaf_ref) = rest[:-4], rest[-4:]
    mine = mine_ref[...]
    build_taps(off_ref, wt_ref, mine, rhs_ref)
    columns = outs[0].shape[1]
    span = (freq_count.bit_length() - 1) * SHIFT
    blocks = convolve(x_ref[...], span, columns, mine[1:2, :], rhs_ref, time_ref, lhs_ref, plane_ref, leaf_ref)
    store_rows(blocks, outs)


def tail_kernel(freq_count, tm_count, x_ref, next_ref, rhs_ref, delay_ref, far_body_ref, *rest):
    outs, far_ref, (time_ref, lhs_ref, plane_ref, leaf_ref) = rest[:-5], rest[-5], rest[-4:]
    tail = outs[0].shape[1]
    body = x_ref.shape[1] - tail
    span = (freq_count.bit_length() - 1) * SHIFT
    inside = lax.axis_index("tm") < tm_count - 1
    following = jnp.where(inside, next_ref[...].astype(jnp.float32), 0.0).astype(jnp.bfloat16)
    window = jnp.concatenate([x_ref[:, body:], following], axis=1)
    blocks = convolve(window, span, tail, delay_ref[1:2, :], rhs_ref, time_ref, lhs_ref, plane_ref, leaf_ref)
    far_ref[:, :body] = far_body_ref[...]
    store_rows(blocks, [*outs, far_ref.at[:, body:]])


def second_half_kernel(body_ref, tail_ref, out_ref):
    piece, _ = out_ref.shape
    body = body_ref.shape[1]
    out_ref[:, :body] = body_ref[piece:, :]
    out_ref[:, body:] = tail_ref[piece:, :]


def final_kernel(*refs):
    own_refs, far_ref, out_ref = refs[:2], refs[-2], refs[-1]
    pair_refs = [refs[k : k + 3] for k in range(2, len(refs) - 2, 3)]
    piece, seg = out_ref.shape
    body = refs[0].shape[1]

    def add_up(first_core):
        for part, columns in ((0, slice(0, body)), (1, slice(body, seg))):
            planes = [own_refs[part][...]]
            for pair in pair_refs:
                here, there = pair[part][:piece, :], pair[2][:, columns]
                planes += [here, there] if first_core else [there, here]
            planes.append(far_ref[:, columns])
            while len(planes) > 1:
                planes = [
                    (lower.astype(jnp.float32) + upper.astype(jnp.float32)).astype(jnp.bfloat16)
                    for lower, upper in zip(planes[::2], planes[1::2])
                ]
            out_ref[:, columns] = planes[0]

    core = lax.axis_index("trial")
    pl.when(core == 0)(lambda: add_up(True))
    pl.when(core != 0)(lambda: add_up(False))


def call(kernel, outs, *args, scratch=(), limit=16 << 20, space=None):
    specs = {} if space is None else {"in_specs": [pl.BlockSpec(memory_space=space)] * len(args)}
    if space is not None:
        args = [pltpu.with_memory_space_constraint(arg, space) for arg in args]
    return pl.pallas_call(
        kernel,
        out_shape=outs,
        **specs,
        scratch_shapes=list(scratch),
        compiler_params=pltpu.CompilerParams(vmem_limit_bytes=limit),
    )(*args)


def plane_of(*shape):
    return jax.ShapeDtypeStruct(shape, jnp.bfloat16)


def shards(spectra, tap_offsets, tap_weights, trial_map, delays):
    band, seg = spectra.shape
    trials = trial_map.shape[1]
    freq_count = lax.axis_size("freq")
    tm_count = lax.axis_size("tm")
    levels = freq_count.bit_length() - 1
    core_count = lax.axis_size("trial")
    rows = trials // core_count
    span = levels * SHIFT
    tail = -(-(MAXOFF - 1 + span) // LANES) * LANES
    body = seg - tail

    def scratch(columns):
        leaf_rows = columns + span
        lhs_rows = leaf_rows + FINE * (PLANES - 1)
        return (
            pltpu.VMEM((lhs_rows + FINE, LANES), jnp.float32),
            pltpu.VMEM((lhs_rows, FINE * band), jnp.bfloat16),
            pltpu.VMEM((lhs_rows, PLANES * rows), jnp.float32),
            pltpu.VMEM((leaf_rows, rows), jnp.float32),
        )

    edge, samples, lags, weights, columns = call(
        functools.partial(load_kernel, freq_count),
        [
            plane_of(band, tail),
            plane_of(band, seg),
            jax.ShapeDtypeStruct((band, trials), jnp.int32),
            plane_of(band, trials),
            jax.ShapeDtypeStruct((8, rows), jnp.int32),
        ],
        spectra,
        jnp.swapaxes(tap_offsets[0], 0, 1),
        jnp.swapaxes(tap_weights[0], 0, 1),
        trial_map,
        delays,
        scratch=(
            pltpu.VMEM((1, trials), jnp.int32),
            pltpu.VMEM(delays.shape, jnp.int32),
            pltpu.SemaphoreType.DMA((5,)),
        ),
        space=pltpu.HBM,
    )
    ring = [
        (((m + 1) % tm_count) * core_count + core_count - 1 - c, m * core_count + c)
        for m in range(tm_count)
        for c in range(core_count)
    ]
    following = lax.ppermute(edge, ("tm", "trial"), ring)
    piece = rows // freq_count
    pairs = shared_pairs(freq_count)
    heights = [piece, *[2 * piece] * len(pairs), piece]
    taps, *bodies = call(
        functools.partial(main_kernel, freq_count),
        [
            plane_of(FINE * band, PLANES * rows),
            *[plane_of(height, body) for height in heights],
        ],
        samples,
        lags,
        weights,
        columns,
        scratch=scratch(body),
    )
    devices = [(f, c) for f in range(freq_count) for c in range(core_count)]

    def traded(blocks):
        arrived = []
        for pair, block in zip(pairs, blocks):
            route = [(f * core_count + c, (f ^ pair[c]) * core_count + c) for f, c in devices]
            arrived.append(lax.ppermute(block, ("freq", "trial"), route))
        return arrived

    own, *bodies, far_body = bodies
    bodies = traded(bodies)
    own_tail, *tails, far = call(
        functools.partial(tail_kernel, freq_count, tm_count),
        [*[plane_of(height, tail) for height in heights[:-1]], plane_of(piece, seg)],
        samples,
        following,
        taps,
        columns,
        far_body,
        scratch=scratch(tail),
    )
    tails = traded(tails)
    route = [(f * core_count + c, (f ^ (freq_count - 1)) * core_count + core_count - 1 - c) for f, c in devices]
    far = lax.ppermute(far, ("freq", "trial"), route)
    received = []
    for both in zip(bodies, tails):
        handed = call(second_half_kernel, plane_of(piece, seg), *both)
        received += [*both, lax.ppermute(handed, "trial", [(0, 1), (1, 0)])]
    return call(final_kernel, plane_of(piece, seg), own, own_tail, *received, far)


def solution(mesh):
    return jax.shard_map(
        shards,
        mesh=mesh,
        in_specs=(
            P(("beam", "freq"), "tm"),
            P("freq", None, None),
            P("freq", None, None),
            P("freq", None),
            P(),
        ),
        out_specs=P(("beam", "freq", "trial"), "tm"),
        check_vma=False,
    )
```

```python
import functools

import jax
import jax.numpy as jnp
from jax import lax
from jax.experimental import pallas as pl
from jax.experimental.pallas import tpu as pltpu
from jax.sharding import PartitionSpec as P


MAXOFF = 32
SHIFT = 32
LANES = 128
FINE = 8
PLANES = (MAXOFF - 1 + FINE - 1) // FINE + 1


def shared_pairs(freq_count):
    return [(r, r + 1) for r in range(1, freq_count - 1, 2)]


def block_order(freq_count, core_index):
    other = 1 - core_index
    order = [(0, core_index)]
    for first, second in shared_pairs(freq_count):
        mine = first + core_index * (second - first)
        order += [(mine, core_index), (mine, other)]
    return [*order, (freq_count - 1, other)]


def own_columns(freq_count, map_ref, del_ref):
    trials = map_ref.shape[1]
    core_count = lax.axis_size("trial")
    row_block = trials // (core_count * freq_count)
    rows = trials // core_count
    levels = freq_count.bit_length() - 1
    freq_index = lax.axis_index("freq")
    core_index = lax.axis_index("trial")
    total = jnp.zeros((1, trials), jnp.int32)
    for level in range(levels):
        first_node = freq_count - (freq_count >> level)
        pair = lax.shift_right_logical(freq_index, level + 1)
        upper = lax.shift_right_logical(freq_index, level) & 1
        for k in range(freq_count >> level + 1):
            total = total + del_ref[first_node + k : first_node + k + 1, :] * jnp.where(pair == k, upper, 0)
    first = lax.broadcasted_iota(jnp.int32, (8, trials), 0) == 0
    both = jnp.where(
        first, jnp.broadcast_to(map_ref[...], (8, trials)), jnp.broadcast_to(total, (8, trials))
    )
    place = lax.broadcasted_iota(jnp.int32, (8, rows), 1) // row_block
    mine = jnp.zeros((8, rows), jnp.int32)
    for position, (distance, core) in enumerate(block_order(freq_count, core_index)):
        start = ((freq_index ^ distance) * core_count + core) * row_block
        turn = lax.rem(position * row_block - start + trials, trials)
        mine = jnp.where(place == position, pltpu.roll(both, turn, 1)[:, :rows], mine)
    return mine


def build_taps(off_ref, wt_ref, mine, rhs_ref):
    band, trials = wt_ref.shape
    rows = mine.shape[1]
    picker = mine[0:1, :] == lax.broadcasted_iota(jnp.int32, (trials, rows), 0)
    picker = picker.astype(jnp.float32).astype(jnp.bfloat16)
    tables = jnp.concatenate([wt_ref[...], off_ref[...].astype(jnp.float32).astype(jnp.bfloat16)], axis=0)
    picked = jnp.dot(tables, picker, preferred_element_type=jnp.float32)
    weights = picked[:band].astype(jnp.bfloat16)
    lags = (picked[band:] + (mine[1:2, :] & (FINE - 1)).astype(jnp.float32)).astype(jnp.bfloat16)
    zero = jnp.zeros_like(weights)
    for fine in range(FINE):
        for plane in range(PLANES):
            rhs_ref[fine * band : (fine + 1) * band, plane * rows : (plane + 1) * rows] = jnp.where(
                lags == plane * FINE + fine, weights, zero
            )


def convolve(window, span, columns, delay_row, rhs_ref, time_ref, lhs_ref, plane_ref, leaf_ref):
    band = window.shape[0]
    rows = delay_row.shape[1]
    leaf_rows = columns + span
    lhs_rows = leaf_rows + FINE * (PLANES - 1)
    time_rows = lhs_rows + FINE
    turned = jnp.transpose(jnp.concatenate([window] * (LANES // band), axis=0)).astype(jnp.float32)
    time_ref[:time_rows, :] = turned[:time_rows, :]
    low_lanes = lax.broadcasted_iota(jnp.int32, (lhs_rows, LANES), 1) < band
    for pair in range(FINE // 2):
        lhs_ref[:lhs_rows, pair * LANES : (pair + 1) * LANES] = jnp.where(
            low_lanes,
            time_ref[2 * pair : 2 * pair + lhs_rows, :],
            time_ref[2 * pair + 1 : 2 * pair + 1 + lhs_rows, :],
        ).astype(jnp.bfloat16)
    plane_ref[:lhs_rows, :] = jnp.dot(lhs_ref[:lhs_rows, :], rhs_ref[...], preferred_element_type=jnp.float32)
    leaf = plane_ref[:leaf_rows, :rows]
    for plane in range(1, PLANES):
        leaf = leaf + plane_ref[plane * FINE : plane * FINE + leaf_rows, plane * rows : (plane + 1) * rows]
    leaf_ref[:leaf_rows, :] = leaf
    steps = [FINE]
    while steps[-1] * 2 <= span:
        steps.append(steps[-1] * 2)
    blocks = []
    for start in range(0, columns, LANES):
        part = leaf_ref[start : start + LANES + span, :]
        for step in reversed(steps):
            length = LANES + sum(s for s in steps if s < step)
            length = min(length, part.shape[0])
            take = jnp.broadcast_to((delay_row & step) != 0, (length, rows))
            moved = part[step : step + length]
            if moved.shape[0] < length:
                moved = jnp.concatenate([moved, jnp.zeros((length - moved.shape[0], rows), jnp.float32)], axis=0)
            part = jnp.where(take, moved, part[:length])
        blocks.append(jnp.transpose(part[:LANES].astype(jnp.bfloat16)))
    return blocks


def store_rows(blocks, outs):
    first = 0
    for out_ref in outs:
        rows = slice(first, first + out_ref.shape[0])
        first += out_ref.shape[0]
        for index, block in enumerate(blocks):
            out_ref[:, index * LANES : (index + 1) * LANES] = block[rows]


def load_kernel(
    freq_count, x_hbm, off_hbm, wt_hbm, map_hbm, del_hbm, edge_ref, x_ref, off_ref, wt_ref, mine_ref, map_ref, del_ref, sems
):
    targets = ((map_hbm, map_ref), (del_hbm, del_ref), (x_hbm, x_ref), (off_hbm, off_ref), (wt_hbm, wt_ref))
    moves = [pltpu.make_async_copy(source, target, sems.at[k]) for k, (source, target) in enumerate(targets)]
    for move in moves:
        move.start()
    for move in moves[:2]:
        move.wait()
    mine_ref[...] = own_columns(freq_count, map_ref, del_ref)
    moves[2].wait()
    edge_ref[...] = x_ref[:, : edge_ref.shape[1]]
    for move in moves[3:]:
        move.wait()


def main_kernel(
    freq_count, x_ref, off_ref, wt_ref, mine_ref, rhs_ref, *rest
):
    outs, (time_ref, lhs_ref, plane_ref, leaf_ref) = rest[:-4], rest[-4:]
    mine = mine_ref[...]
    build_taps(off_ref, wt_ref, mine, rhs_ref)
    columns = outs[0].shape[1]
    span = (freq_count.bit_length() - 1) * SHIFT
    blocks = convolve(x_ref[...], span, columns, mine[1:2, :], rhs_ref, time_ref, lhs_ref, plane_ref, leaf_ref)
    store_rows(blocks, outs)


def tail_kernel(freq_count, tm_count, x_ref, next_ref, rhs_ref, delay_ref, far_body_ref, *rest):
    outs, far_ref, (time_ref, lhs_ref, plane_ref, leaf_ref) = rest[:-5], rest[-5], rest[-4:]
    tail = outs[0].shape[1]
    body = x_ref.shape[1] - tail
    span = (freq_count.bit_length() - 1) * SHIFT
    inside = lax.axis_index("tm") < tm_count - 1
    following = jnp.where(inside, next_ref[...].astype(jnp.float32), 0.0).astype(jnp.bfloat16)
    window = jnp.concatenate([x_ref[:, body:], following], axis=1)
    blocks = convolve(window, span, tail, delay_ref[1:2, :], rhs_ref, time_ref, lhs_ref, plane_ref, leaf_ref)
    far_ref[:, :body] = far_body_ref[...]
    store_rows(blocks, [*outs, far_ref.at[:, body:]])


def second_half_kernel(body_ref, tail_ref, out_ref):
    piece, _ = out_ref.shape
    body = body_ref.shape[1]
    out_ref[:, :body] = body_ref[piece:, :]
    out_ref[:, body:] = tail_ref[piece:, :]


def final_kernel(*refs):
    own_refs, far_ref, out_ref = refs[:2], refs[-2], refs[-1]
    pair_refs = [refs[k : k + 3] for k in range(2, len(refs) - 2, 3)]
    piece, seg = out_ref.shape
    body = refs[0].shape[1]

    def add_up(first_core):
        for part, columns in ((0, slice(0, body)), (1, slice(body, seg))):
            planes = [own_refs[part][...]]
            for pair in pair_refs:
                here, there = pair[part][:piece, :], pair[2][:, columns]
                planes += [here, there] if first_core else [there, here]
            planes.append(far_ref[:, columns])
            while len(planes) > 1:
                planes = [
                    (lower.astype(jnp.float32) + upper.astype(jnp.float32)).astype(jnp.bfloat16)
                    for lower, upper in zip(planes[::2], planes[1::2])
                ]
            out_ref[:, columns] = planes[0]

    core = lax.axis_index("trial")
    pl.when(core == 0)(lambda: add_up(True))
    pl.when(core != 0)(lambda: add_up(False))


def call(kernel, outs, *args, scratch=(), limit=16 << 20, space=None):
    specs = {} if space is None else {"in_specs": [pl.BlockSpec(memory_space=space)] * len(args)}
    if space is not None:
        args = [pltpu.with_memory_space_constraint(arg, space) for arg in args]
    return pl.pallas_call(
        kernel,
        out_shape=outs,
        **specs,
        scratch_shapes=list(scratch),
        compiler_params=pltpu.CompilerParams(vmem_limit_bytes=limit),
    )(*args)


def plane_of(*shape):
    return jax.ShapeDtypeStruct(shape, jnp.bfloat16)


def shards(spectra, tap_offsets, tap_weights, trial_map, delays):
    band, seg = spectra.shape
    trials = trial_map.shape[1]
    freq_count = lax.axis_size("freq")
    tm_count = lax.axis_size("tm")
    levels = freq_count.bit_length() - 1
    core_count = lax.axis_size("trial")
    rows = trials // core_count
    span = levels * SHIFT
    tail = -(-(MAXOFF - 1 + span) // LANES) * LANES
    body = seg - tail

    def scratch(columns):
        leaf_rows = columns + span
        lhs_rows = leaf_rows + FINE * (PLANES - 1)
        return (
            pltpu.VMEM((lhs_rows + FINE, LANES), jnp.float32),
            pltpu.VMEM((lhs_rows, FINE * band), jnp.bfloat16),
            pltpu.VMEM((lhs_rows, PLANES * rows), jnp.float32),
            pltpu.VMEM((leaf_rows, rows), jnp.float32),
        )

    edge, samples, lags, weights, columns = call(
        functools.partial(load_kernel, freq_count),
        [
            plane_of(band, tail),
            plane_of(band, seg),
            jax.ShapeDtypeStruct((band, trials), jnp.int32),
            plane_of(band, trials),
            jax.ShapeDtypeStruct((8, rows), jnp.int32),
        ],
        spectra,
        jnp.swapaxes(tap_offsets[0], 0, 1),
        jnp.swapaxes(tap_weights[0], 0, 1),
        trial_map,
        delays,
        scratch=(
            pltpu.VMEM((1, trials), jnp.int32),
            pltpu.VMEM(delays.shape, jnp.int32),
            pltpu.SemaphoreType.DMA((5,)),
        ),
        space=pltpu.HBM,
    )
    ring = [
        (((m + 1) % tm_count) * core_count + core_count - 1 - c, m * core_count + c)
        for m in range(tm_count)
        for c in range(core_count)
    ]
    following = lax.ppermute(edge, ("tm", "trial"), ring)
    piece = rows // freq_count
    pairs = shared_pairs(freq_count)
    heights = [piece, *[2 * piece] * len(pairs), piece]
    taps, *bodies = call(
        functools.partial(main_kernel, freq_count),
        [
            plane_of(FINE * band, PLANES * rows),
            *[plane_of(height, body) for height in heights],
        ],
        samples,
        lags,
        weights,
        columns,
        scratch=scratch(body),
    )
    devices = [(f, c) for f in range(freq_count) for c in range(core_count)]

    def traded(blocks):
        arrived = []
        for pair, block in zip(pairs, blocks):
            route = [(f * core_count + c, (f ^ pair[c]) * core_count + c) for f, c in devices]
            arrived.append(lax.ppermute(block, ("freq", "trial"), route))
        return arrived

    own, *bodies, far_body = bodies
    bodies = traded(bodies)
    own_tail, *tails, far = call(
        functools.partial(tail_kernel, freq_count, tm_count),
        [*[plane_of(height, tail) for height in heights[:-1]], plane_of(piece, seg)],
        samples,
        following,
        taps,
        columns,
        far_body,
        scratch=scratch(tail),
    )
    tails = traded(tails)
    route = [(f * core_count + c, (f ^ (freq_count - 1)) * core_count + core_count - 1 - c) for f, c in devices]
    far = lax.ppermute(far, ("freq", "trial"), route)
    received = []
    for both in zip(bodies, tails):
        handed = call(second_half_kernel, plane_of(piece, seg), *both)
        received += [*both, lax.ppermute(handed, "trial", [(0, 1), (1, 0)])]
    return call(final_kernel, plane_of(piece, seg), own, own_tail, *received, far)


def solution(mesh):
    return jax.shard_map(
        shards,
        mesh=mesh,
        in_specs=(
            P(("beam", "freq"), "tm"),
            P("freq", None, None),
            P("freq", None, None),
            P("freq", None),
            P(),
        ),
        out_specs=P(("beam", "freq", "trial"), "tm"),
        check_vma=False,
    )
```

```python
import functools

import jax
import jax.numpy as jnp
from jax import lax
from jax.experimental import pallas as pl
from jax.experimental.pallas import tpu as pltpu
from jax.sharding import PartitionSpec as P


MAXOFF = 32
SHIFT = 32
LANES = 128
FINE = 4
SUBLANES = 8
PLANES = (MAXOFF - 1 + FINE - 1) // FINE + 1


def shared_pairs(freq_count):
    return [(r, r + 1) for r in range(1, freq_count - 1, 2)]


def block_order(freq_count, core_index):
    other = 1 - core_index
    order = [(0, core_index)]
    for first, second in shared_pairs(freq_count):
        mine = first + core_index * (second - first)
        order += [(mine, core_index), (mine, other)]
    return [*order, (freq_count - 1, other)]


def own_columns(freq_count, map_ref, del_ref):
    trials = map_ref.shape[1]
    core_count = lax.axis_size("trial")
    row_block = trials // (core_count * freq_count)
    rows = trials // core_count
    levels = freq_count.bit_length() - 1
    freq_index = lax.axis_index("freq")
    core_index = lax.axis_index("trial")
    total = jnp.zeros((1, trials), jnp.int32)
    for level in range(levels):
        first_node = freq_count - (freq_count >> level)
        pair = lax.shift_right_logical(freq_index, level + 1)
        upper = lax.shift_right_logical(freq_index, level) & 1
        for k in range(freq_count >> level + 1):
            total = total + del_ref[first_node + k : first_node + k + 1, :] * jnp.where(pair == k, upper, 0)
    first = lax.broadcasted_iota(jnp.int32, (8, trials), 0) == 0
    both = jnp.where(
        first, jnp.broadcast_to(map_ref[...], (8, trials)), jnp.broadcast_to(total, (8, trials))
    )
    place = lax.broadcasted_iota(jnp.int32, (8, rows), 1) // row_block
    mine = jnp.zeros((8, rows), jnp.int32)
    for position, (distance, core) in enumerate(block_order(freq_count, core_index)):
        start = ((freq_index ^ distance) * core_count + core) * row_block
        turn = lax.rem(position * row_block - start + trials, trials)
        mine = jnp.where(place == position, pltpu.roll(both, turn, 1)[:, :rows], mine)
    return mine


def build_taps(off_ref, wt_ref, mine, rhs_ref):
    band, trials = wt_ref.shape
    rows = mine.shape[1]
    picker = mine[0:1, :] == lax.broadcasted_iota(jnp.int32, (trials, rows), 0)
    picker = picker.astype(jnp.float32).astype(jnp.bfloat16)
    tables = jnp.concatenate([wt_ref[...], off_ref[...].astype(jnp.float32).astype(jnp.bfloat16)], axis=0)
    picked = jnp.dot(tables, picker, preferred_element_type=jnp.float32)
    weights = picked[:band].astype(jnp.bfloat16)
    lags = (picked[band:] + (mine[1:2, :] & (FINE - 1)).astype(jnp.float32)).astype(jnp.bfloat16)
    zero = jnp.zeros_like(weights)
    for fine in range(FINE):
        for plane in range(PLANES):
            rhs_ref[fine * band : (fine + 1) * band, plane * rows : (plane + 1) * rows] = jnp.where(
                lags == plane * FINE + fine, weights, zero
            )


def convolve(window, span, columns, delay_row, rhs_ref, time_ref, lhs_ref, plane_ref, leaf_ref):
    band = window.shape[0]
    rows = delay_row.shape[1]
    leaf_rows = columns + span
    lhs_rows = leaf_rows + FINE * (PLANES - 1)
    time_rows = lhs_rows + SUBLANES
    turned = jnp.transpose(jnp.concatenate([window] * (LANES // band), axis=0)).astype(jnp.float32)
    time_ref[:time_rows, :] = turned[:time_rows, :]
    low_lanes = lax.broadcasted_iota(jnp.int32, (lhs_rows, LANES), 1) < band
    for pair in range(FINE // 2):
        lhs_ref[:lhs_rows, pair * LANES : (pair + 1) * LANES] = jnp.where(
            low_lanes,
            time_ref[2 * pair : 2 * pair + lhs_rows, :],
            time_ref[2 * pair + 1 : 2 * pair + 1 + lhs_rows, :],
        ).astype(jnp.bfloat16)
    plane_ref[:lhs_rows, :] = jnp.dot(lhs_ref[:lhs_rows, :], rhs_ref[...], preferred_element_type=jnp.float32)
    leaf = plane_ref[:leaf_rows, :rows]
    for plane in range(1, PLANES):
        leaf = leaf + plane_ref[plane * FINE : plane * FINE + leaf_rows, plane * rows : (plane + 1) * rows]
    leaf_ref[:leaf_rows, :] = leaf
    steps = [FINE]
    while steps[-1] * 2 <= span:
        steps.append(steps[-1] * 2)
    blocks = []
    for start in range(0, columns, LANES):
        part = leaf_ref[start : start + LANES + span, :]
        for step in reversed(steps):
            length = LANES + sum(s for s in steps if s < step)
            length = min(length, part.shape[0])
            take = jnp.broadcast_to((delay_row & step) != 0, (length, rows))
            moved = part[step : step + length]
            if moved.shape[0] < length:
                moved = jnp.concatenate([moved, jnp.zeros((length - moved.shape[0], rows), jnp.float32)], axis=0)
            part = jnp.where(take, moved, part[:length])
        blocks.append(jnp.transpose(part[:LANES].astype(jnp.bfloat16)))
    return blocks


def store_rows(blocks, outs):
    first = 0
    for out_ref in outs:
        rows = slice(first, first + out_ref.shape[0])
        first += out_ref.shape[0]
        for index, block in enumerate(blocks):
            out_ref[:, index * LANES : (index + 1) * LANES] = block[rows]


def load_kernel(
    freq_count, x_hbm, off_hbm, wt_hbm, map_hbm, del_hbm, edge_ref, x_ref, off_ref, wt_ref, mine_ref, map_ref, del_ref, sems
):
    targets = ((map_hbm, map_ref), (del_hbm, del_ref), (x_hbm, x_ref), (off_hbm, off_ref), (wt_hbm, wt_ref))
    moves = [pltpu.make_async_copy(source, target, sems.at[k]) for k, (source, target) in enumerate(targets)]
    for move in moves:
        move.start()
    for move in moves[:2]:
        move.wait()
    mine_ref[...] = own_columns(freq_count, map_ref, del_ref)
    moves[2].wait()
    edge_ref[...] = x_ref[:, : edge_ref.shape[1]]
    for move in moves[3:]:
        move.wait()


def main_kernel(
    freq_count, x_ref, off_ref, wt_ref, mine_ref, rhs_ref, *rest
):
    outs, (time_ref, lhs_ref, plane_ref, leaf_ref) = rest[:-4], rest[-4:]
    mine = mine_ref[...]
    build_taps(off_ref, wt_ref, mine, rhs_ref)
    columns = outs[0].shape[1]
    span = (freq_count.bit_length() - 1) * SHIFT
    blocks = convolve(x_ref[...], span, columns, mine[1:2, :], rhs_ref, time_ref, lhs_ref, plane_ref, leaf_ref)
    store_rows(blocks, outs)


def tail_kernel(freq_count, tm_count, x_ref, next_ref, rhs_ref, delay_ref, far_body_ref, *rest):
    outs, far_ref, (time_ref, lhs_ref, plane_ref, leaf_ref) = rest[:-5], rest[-5], rest[-4:]
    tail = outs[0].shape[1]
    body = x_ref.shape[1] - tail
    span = (freq_count.bit_length() - 1) * SHIFT
    inside = lax.axis_index("tm") < tm_count - 1
    following = jnp.where(inside, next_ref[...].astype(jnp.float32), 0.0).astype(jnp.bfloat16)
    window = jnp.concatenate([x_ref[:, body:], following], axis=1)
    blocks = convolve(window, span, tail, delay_ref[1:2, :], rhs_ref, time_ref, lhs_ref, plane_ref, leaf_ref)
    far_ref[:, :body] = far_body_ref[...]
    store_rows(blocks, [*outs, far_ref.at[:, body:]])


def second_half_kernel(body_ref, tail_ref, out_ref):
    piece, _ = out_ref.shape
    body = body_ref.shape[1]
    out_ref[:, :body] = body_ref[piece:, :]
    out_ref[:, body:] = tail_ref[piece:, :]


def final_kernel(*refs):
    own_refs, far_ref, out_ref = refs[:2], refs[-2], refs[-1]
    pair_refs = [refs[k : k + 3] for k in range(2, len(refs) - 2, 3)]
    piece, seg = out_ref.shape
    body = refs[0].shape[1]

    def add_up(first_core):
        for part, columns in ((0, slice(0, body)), (1, slice(body, seg))):
            planes = [own_refs[part][...]]
            for pair in pair_refs:
                here, there = pair[part][:piece, :], pair[2][:, columns]
                planes += [here, there] if first_core else [there, here]
            planes.append(far_ref[:, columns])
            while len(planes) > 1:
                planes = [
                    (lower.astype(jnp.float32) + upper.astype(jnp.float32)).astype(jnp.bfloat16)
                    for lower, upper in zip(planes[::2], planes[1::2])
                ]
            out_ref[:, columns] = planes[0]

    core = lax.axis_index("trial")
    pl.when(core == 0)(lambda: add_up(True))
    pl.when(core != 0)(lambda: add_up(False))


def call(kernel, outs, *args, scratch=(), limit=16 << 20, space=None):
    specs = {} if space is None else {"in_specs": [pl.BlockSpec(memory_space=space)] * len(args)}
    if space is not None:
        args = [pltpu.with_memory_space_constraint(arg, space) for arg in args]
    return pl.pallas_call(
        kernel,
        out_shape=outs,
        **specs,
        scratch_shapes=list(scratch),
        compiler_params=pltpu.CompilerParams(vmem_limit_bytes=limit),
    )(*args)


def plane_of(*shape):
    return jax.ShapeDtypeStruct(shape, jnp.bfloat16)


def shards(spectra, tap_offsets, tap_weights, trial_map, delays):
    band, seg = spectra.shape
    trials = trial_map.shape[1]
    freq_count = lax.axis_size("freq")
    tm_count = lax.axis_size("tm")
    levels = freq_count.bit_length() - 1
    core_count = lax.axis_size("trial")
    rows = trials // core_count
    span = levels * SHIFT
    tail = -(-(span + FINE * (PLANES - 1) + SUBLANES) // LANES) * LANES
    body = seg - tail

    def scratch(columns):
        leaf_rows = columns + span
        lhs_rows = leaf_rows + FINE * (PLANES - 1)
        return (
            pltpu.VMEM((lhs_rows + SUBLANES, LANES), jnp.float32),
            pltpu.VMEM((lhs_rows, FINE * band), jnp.bfloat16),
            pltpu.VMEM((lhs_rows, PLANES * rows), jnp.float32),
            pltpu.VMEM((leaf_rows, rows), jnp.float32),
        )

    edge, samples, lags, weights, columns = call(
        functools.partial(load_kernel, freq_count),
        [
            plane_of(band, tail),
            plane_of(band, seg),
            jax.ShapeDtypeStruct((band, trials), jnp.int32),
            plane_of(band, trials),
            jax.ShapeDtypeStruct((8, rows), jnp.int32),
        ],
        spectra,
        jnp.swapaxes(tap_offsets[0], 0, 1),
        jnp.swapaxes(tap_weights[0], 0, 1),
        trial_map,
        delays,
        scratch=(
            pltpu.VMEM((1, trials), jnp.int32),
            pltpu.VMEM(delays.shape, jnp.int32),
            pltpu.SemaphoreType.DMA((5,)),
        ),
        space=pltpu.HBM,
    )
    ring = [
        (((m + 1) % tm_count) * core_count + core_count - 1 - c, m * core_count + c)
        for m in range(tm_count)
        for c in range(core_count)
    ]
    following = lax.ppermute(edge, ("tm", "trial"), ring)
    piece = rows // freq_count
    pairs = shared_pairs(freq_count)
    heights = [piece, *[2 * piece] * len(pairs), piece]
    taps, *bodies = call(
        functools.partial(main_kernel, freq_count),
        [
            plane_of(FINE * band, PLANES * rows),
            *[plane_of(height, body) for height in heights],
        ],
        samples,
        lags,
        weights,
        columns,
        scratch=scratch(body),
    )
    devices = [(f, c) for f in range(freq_count) for c in range(core_count)]

    def traded(blocks):
        arrived = []
        for pair, block in zip(pairs, blocks):
            route = [(f * core_count + c, (f ^ pair[c]) * core_count + c) for f, c in devices]
            arrived.append(lax.ppermute(block, ("freq", "trial"), route))
        return arrived

    own, *bodies, far_body = bodies
    bodies = traded(bodies)
    own_tail, *tails, far = call(
        functools.partial(tail_kernel, freq_count, tm_count),
        [*[plane_of(height, tail) for height in heights[:-1]], plane_of(piece, seg)],
        samples,
        following,
        taps,
        columns,
        far_body,
        scratch=scratch(tail),
    )
    tails = traded(tails)
    route = [(f * core_count + c, (f ^ (freq_count - 1)) * core_count + core_count - 1 - c) for f, c in devices]
    far = lax.ppermute(far, ("freq", "trial"), route)
    received = []
    for both in zip(bodies, tails):
        handed = call(second_half_kernel, plane_of(piece, seg), *both)
        received += [*both, lax.ppermute(handed, "trial", [(0, 1), (1, 0)])]
    return call(final_kernel, plane_of(piece, seg), own, own_tail, *received, far)


def solution(mesh):
    return jax.shard_map(
        shards,
        mesh=mesh,
        in_specs=(
            P(("beam", "freq"), "tm"),
            P("freq", None, None),
            P("freq", None, None),
            P("freq", None),
            P(),
        ),
        out_specs=P(("beam", "freq", "trial"), "tm"),
        check_vma=False,
    )
```
